32 devices in a mesh: va: 8 (over z, y), vb: 4 (over x, core).
Axes of the slice: x: 2, y: 2, z: 4, core: 2. Of those that a mesh axis runs over, the one named last changes fastest.
Arguments:
- amplitudes: bfloat16 [2, 2, 2048, 2048], P(None, None, 'va', 'vb'), may hold values from -6 to 6
- integrals: bfloat16 [4, 2048, 2048], P(None, 'va', 'vb'), may hold values from -0.125 to 0.125
- occ_energy: float32 [2], replicated, may hold values from -2 to -0.5
- vir_energy: float32 [2048], replicated, may hold values from 0.2 to 3
- screen: int32 [8, 8], replicated, may hold values from -1 to 15, as said below
- lengths: int32 [8], replicated, may hold values from 2 to 8, as said below
Outputs:
- update: float32 [2, 2, 2048, 2048], P(None, None, 'va', 'vb')
The draws below stay inside these ranges and needn't reach their ends.
Inputs may be any that keep to these rules, and one draw needn't show every extreme that they name: `screen`: row r holds lengths[r] distinct tile numbers below 16 in its first slots and -1 in the others. `lengths`: exactly one grid row lists 8 tiles; every other row lists at most 4.
All inputs are finite; a program needn't handle non-finite values.
Results may differ from the reference program's by a relative error of at most 0.0031.
Values may be sent and summed in bfloat16 or wider, within the bound.
A program may use at most 64 MiB of HBM per device.

```python
import jax
import jax.numpy as jnp
from jax import lax

V = 2048
TILE = 128
OCC = 2
LIST = 8
TILES = 16
N_VA = 8


def screened_rows(key):
    base = jax.random.fold_in(key, 7)
    key_len, key_row, key_perm = jax.random.split(base, 3)
    row_lens = jax.random.randint(key_len, (N_VA,), 2, LIST // 2 + 1)
    full_row = jax.random.randint(key_row, (), 0, N_VA)
    row_lens = jnp.where(jnp.arange(N_VA) == full_row, LIST, row_lens).astype(jnp.int32)
    row_keys = jax.random.split(key_perm, N_VA)
    shuffled = jax.vmap(lambda one_key: jax.random.permutation(one_key, TILES))(row_keys)[:, :LIST]
    tile_ids = jnp.where(jnp.arange(LIST)[None, :] < row_lens[:, None], shuffled, -1).astype(jnp.int32)
    return (tile_ids, row_lens)


def draw_screen(key, part):
    return screened_rows(key)[0]


def draw_lengths(key, part):
    return screened_rows(key)[1]


def block_scale(own_key, dims, pieces, low, largest):
    def one(position, blocks):
        steps = jax.random.uniform(jax.random.fold_in(jax.random.fold_in(own_key, 6), position), (blocks,), jnp.float32, low / len(pieces), largest / len(pieces))
        return jnp.repeat(jnp.exp(steps), dims[position] // blocks).reshape((-1,) + (1,) * (len(dims) - position - 1))

    factor_of = one(*pieces[0])
    for cut in pieces[1:]:
        factor_of = factor_of * one(*cut)
    return factor_of


def noise(rng, dims, scale, most, pieces=(), kind=jnp.bfloat16):
    result = scale * jax.random.normal(rng, dims, jnp.float32)
    if pieces:
        result = result * block_scale(rng, dims, pieces, -0.22, 0.18)
    return jnp.clip(result, -most, most).astype(kind)


def setup_inputs(seed: int = 0) -> dict:
    key_of = jax.random.split(jax.random.key(seed), 7)
    amplitudes = noise(key_of[0], (OCC, OCC, V, V), 1.0, 6.0, ((2, 8), (3, 4)))
    integrals = noise(key_of[1], (OCC * OCC, V, V), (OCC * LIST * TILE) ** -0.5, 0.125, ((1, 8), (2, 4)))
    occ_energy = jnp.clip(jax.random.uniform(key_of[2], (OCC,), jnp.float32, -2.0, -0.5), -2.0, -0.5)
    vir_energy = jnp.clip(jax.random.uniform(key_of[3], (V,), jnp.float32, 0.2, 3.0), 0.2, 3.0)
    screen = draw_screen(jax.random.fold_in(key_of[6], 71), 0)
    lengths = draw_lengths(jax.random.fold_in(key_of[6], 71), 0)
    return dict(amplitudes=amplitudes, integrals=integrals, occ_energy=occ_energy, vir_energy=vir_energy, screen=screen, lengths=lengths)


def reference(amplitudes, integrals, occ_energy, vir_energy, screen, lengths):
    row_len = V // N_VA
    slots = screen.shape[1]
    offsets = jnp.arange(TILE, dtype=jnp.int32)
    blocks = integrals.reshape(OCC, OCC, V, V)

    def row_term(grid_row):
        begin_at = (grid_row * row_len).astype(jnp.int32)
        own_rows = lax.dynamic_slice_in_dim(amplitudes, begin_at, row_len, 2).astype(jnp.float32)
        mirror = jnp.swapaxes(lax.dynamic_slice_in_dim(amplitudes, begin_at, row_len, 3), 2, 3).astype(jnp.float32)
        spin_amp = (2.0 * own_rows - mirror).astype(jnp.bfloat16)
        tile_ids = jnp.maximum(screen[grid_row], 0).astype(jnp.int32)
        is_live = jnp.arange(slots, dtype=jnp.int32) < lengths[grid_row]
        columns = (tile_ids[:, None] * TILE + offsets[None, :]).reshape(-1).astype(jnp.int32)
        picked = jnp.take(spin_amp, columns, axis=3).astype(jnp.float32)
        k_rows = jnp.take(blocks, columns, axis=2).astype(jnp.float32)
        keep_cols = jnp.repeat(is_live, TILE).astype(jnp.float32)
        k_rows = k_rows * keep_cols[None, None, :, None]
        return jnp.einsum("ikac,kjcb->ijab", picked, k_rows, precision=lax.Precision.HIGHEST)

    cycle = lax.map(row_term, jnp.arange(N_VA, dtype=jnp.int32))
    cycle = jnp.transpose(cycle, (1, 2, 0, 3, 4)).reshape(OCC, OCC, V, V)
    denominator = (occ_energy[:, None, None, None] + occ_energy[None, :, None, None]
                   - vir_energy[None, None, :, None] - vir_energy[None, None, None, :])
    return cycle / denominator
```

```python
import functools

import jax
import jax.numpy as jnp
from jax import lax
from jax.experimental import pallas as pl
from jax.experimental.pallas import tpu as pltpu
from jax.sharding import PartitionSpec as P

TILE = 128
PAIR = 2
SPLIT = 2
GROUP = 2
MESH = pl.DeviceIdType.MESH


def gather_kernel(
    count_va, count_vb, flip, amp_ref, *refs
):
    refs = list(refs)
    turned_ref = None if flip else refs.pop(0)
    (
        int_ref, whole_k, spin_all,
        landed, passing, spin, z_send, z_recv, y_send, y_recv, m_send, m_recv, x_send, x_recv, s_send, s_recv, own_sem,
    ) = refs
    va = lax.axis_index("va")
    vb = lax.axis_index("vb")
    ratio = count_va // count_vb
    lines = count_va // PAIR
    outers = count_vb // PAIR
    line, side = va // PAIR, va % PAIR
    outer, core = vb // PAIR, vb % PAIR
    blocks, rows, _ = int_ref.shape
    part_rows = rows // SPLIT
    chunks = blocks * SPLIT
    early = chunks - 1
    halves = amp_ref.shape[0]
    row_len = amp_ref.shape[2]

    def k_slot(owner, chunk):
        begin = owner * rows + chunk % SPLIT * part_rows
        return whole_k.at[chunk // SPLIT, pl.ds(pl.multiple_of(begin, part_rows), part_rows)]

    def own_slot(chunk):
        return int_ref.at[chunk // SPLIT, pl.ds(chunk % SPLIT * part_rows, part_rows)]

    def remote(src, dst, send, recv, target):
        return pltpu.make_async_remote_copy(
            src_ref=src, dst_ref=dst, send_sem=send, recv_sem=recv, device_id=target, device_id_type=MESH
        )

    next_vb = lax.rem(outer + 1, outers) * PAIR + core
    last_vb = lax.rem(outer + outers - 1, outers) * PAIR + core

    def by_relay(half):
        return outers > 1 and half % 2 == 1

    def piece(part):
        if flip:
            return amp_ref.at[:, :, :, pl.ds(part * row_len, row_len)]
        return turned_ref.at[part]

    def half_piece(part, half):
        if flip:
            return amp_ref.at[half, :, :, pl.ds(part * row_len, row_len)]
        return turned_ref.at[part, half]

    def mirror_own(part):
        return pltpu.make_async_copy(piece(part), landed.at[part], own_sem.at[part])

    def mirror_straight(part, half):
        return remote(
            half_piece(part, half), landed.at[va % ratio, half],
            m_send.at[0, part, half], m_recv.at[va % ratio, half],
            {"va": vb * ratio + part, "vb": va // ratio},
        )

    def mirror_out(part, half):
        return remote(
            half_piece(part, half), passing.at[part, half],
            x_send.at[part, half], x_recv.at[part, half], {"vb": next_vb},
        )

    def mirror_on(part, half):
        return remote(
            passing.at[part, half], landed.at[va % ratio, half],
            m_send.at[1, part, half], m_recv.at[va % ratio, half],
            {"va": last_vb * ratio + part, "vb": va // ratio},
        )

    def mirror_passing(part, half):
        here = passing.at[part, half]
        return remote(here, here, x_send.at[part, half], x_recv.at[part, half], {"vb": vb})

    def mirror_arrival(part, half):
        here = landed.at[part, half]
        return remote(here, here, m_send.at[0, part, half], m_recv.at[part, half], {"vb": vb})

    def stays(part):
        return va == vb * ratio + part

    def last_stays(part):
        return va == last_vb * ratio + part

    def each_mirror(own, straight, out):
        for part in range(ratio):

            @pl.when(stays(part))
            def _():
                own(part)

            @pl.when(jnp.logical_not(stays(part)))
            def _():
                for half in range(halves):
                    (out if by_relay(half) else straight)(part, half)

    each_mirror(
        lambda part: mirror_own(part).start(),
        lambda part, half: mirror_straight(part, half).start(),
        lambda part, half: mirror_out(part, half).start(),
    )

    def each_passing(act):
        for part in range(ratio):

            @pl.when(jnp.logical_not(last_stays(part)))
            def _():
                for half in range(halves):
                    if by_relay(half):
                        act(part, half)

    def source(direction, step):
        return line - step if direction == 0 else line + step

    def line_slot(direction, step, chunk):
        if chunk == chunks:
            return k_slot(source(direction, step) * PAIR + 1 - side, early)
        return k_slot(source(direction, step) * PAIR + side, chunk)

    def block_at(direction, step, chunk):
        if step == 0 and chunk < chunks:
            return own_slot(chunk)
        return line_slot(direction, step, chunk)

    def line_send(direction, step, chunk):
        to = line + 1 if direction == 0 else line - 1
        return remote(
            block_at(direction, step, chunk),
            line_slot(direction, step, chunk),
            z_send.at[direction, step, chunk],
            z_recv.at[direction, step, chunk],
            {"va": to * PAIR + side},
        )

    def line_arrival(direction, step, chunk):
        here = line_slot(direction, step, chunk)
        return remote(
            here, here, z_send.at[direction, step - 1, chunk], z_recv.at[direction, step - 1, chunk],
            {"va": va},
        )

    def may_send(direction, step):
        if direction == 0:
            return jnp.logical_and(line - step >= 0, line + 1 < lines)
        return jnp.logical_and(line + step < lines, line - 1 >= 0)

    def has_arrival(direction, step):
        return line - step >= 0 if direction == 0 else line + step < lines

    def side_send(direction, step, chunk):
        return remote(
            block_at(direction, step, chunk),
            line_slot(direction, step, chunk),
            y_send.at[direction, step, chunk],
            y_recv.at[direction, step, chunk],
            {"va": line * PAIR + 1 - side},
        )

    def side_arrival(direction, step, chunk):
        here = k_slot(source(direction, step) * PAIR + 1 - side, chunk)
        return remote(
            here, here, y_send.at[direction, step, chunk], y_recv.at[direction, step, chunk], {"va": va}
        )

    def own_copy(chunk):
        return pltpu.make_async_copy(own_slot(chunk), k_slot(va, chunk), own_sem.at[ratio + 1 + chunk])

    def send_own(chunk):
        for direction in range(2):

            @pl.when(may_send(direction, 0))
            def _():
                line_send(direction, 0, chunk).start()

    side_send(0, 0, early).start()
    for chunk in range(chunks):
        send_own(chunk)
        if chunk != early:
            side_send(0, 0, chunk).start()
    for chunk in range(chunks):
        own_copy(chunk).start()
    side_arrival(0, 0, early).wait_recv()
    send_own(chunks)

    def pass_mirror(part, half):
        mirror_passing(part, half).wait_recv()
        mirror_on(part, half).start()

    each_passing(pass_mirror)

    def line_step(step):
        for chunk in range(chunks + 1):
            for direction in range(2):

                @pl.when(has_arrival(direction, step))
                def _():
                    line_arrival(direction, step, chunk).wait_recv()

                    @pl.when(may_send(direction, step))
                    def _():
                        line_send(direction, step, chunk).start()

                    if chunk < early:
                        side_send(direction, step, chunk).start()

    def spin_send(shift):
        to = lax.rem(outer + shift, outers)
        return remote(
            spin, spin_all.at[vb], s_send.at[0, shift], s_recv.at[0, shift], {"vb": to * PAIR + core}
        )

    def spin_arrival(shift):
        here = spin_all.at[lax.rem(outer + outers - shift, outers) * PAIR + core]
        return remote(here, here, s_send.at[0, shift], s_recv.at[0, shift], {"vb": vb})

    def spin_relay(shift):
        held = spin_all.at[lax.rem(outer + outers - shift, outers) * PAIR + core]
        src = spin if shift == 0 else held
        return remote(
            src, held, s_send.at[1, shift], s_recv.at[1, shift], {"vb": outer * PAIR + 1 - core}
        )

    def relay_arrival(shift):
        here = spin_all.at[lax.rem(outer + outers - shift, outers) * PAIR + 1 - core]
        return remote(here, here, s_send.at[1, shift], s_recv.at[1, shift], {"vb": vb})

    def spin_own():
        return pltpu.make_async_copy(spin, spin_all.at[vb], own_sem.at[ratio])

    def spin_step():
        for part in range(ratio):

            @pl.when(stays(part))
            def _():
                mirror_own(part).wait()

            @pl.when(jnp.logical_not(stays(part)))
            def _():
                for half in range(halves):
                    mirror_arrival(part, half).wait_recv()

            cols = slice(part * row_len, (part + 1) * row_len)
            for i in range(halves):
                for k in range(amp_ref.shape[1]):
                    mirror = landed[part, i, k].astype(jnp.float32)
                    spin[i, k, :, cols] = (
                        2.0 * amp_ref[i, k, :, cols].astype(jnp.float32) - (mirror.T if flip else mirror)
                    ).astype(spin.dtype)
        for shift in range(1, outers):
            spin_send(shift).start()
        spin_relay(0).start()
        spin_own().start()

    spin_after = 1
    for step in range(1, lines):
        line_step(step)
        if step == spin_after:
            spin_step()
    if spin_after == 0:
        spin_step()
    for shift in range(1, outers):
        spin_arrival(shift).wait_recv()
        spin_relay(shift).start()

    for chunk in range(chunks + 1):
        if chunk < chunks:
            own_copy(chunk).wait()
            side_send(0, 0, chunk).wait_send()
            if chunk != early:
                side_arrival(0, 0, chunk).wait_recv()
        for direction in range(2):

            @pl.when(may_send(direction, 0))
            def _():
                line_send(direction, 0, chunk).wait_send()

    for step in range(1, lines):
        for chunk in range(chunks + 1):
            for direction in range(2):

                @pl.when(may_send(direction, step))
                def _():
                    line_send(direction, step, chunk).wait_send()

                if chunk < early:

                    @pl.when(has_arrival(direction, step))
                    def _():
                        side_arrival(direction, step, chunk).wait_recv()
                        side_send(direction, step, chunk).wait_send()

    each_mirror(
        lambda part: None,
        lambda part, half: mirror_straight(part, half).wait_send(),
        lambda part, half: mirror_out(part, half).wait_send(),
    )
    each_passing(lambda part, half: mirror_on(part, half).wait_send())

    spin_own().wait()
    for shift in range(outers):
        relay_arrival(shift).wait_recv()
        spin_relay(shift).wait_send()
    for shift in range(1, outers):
        spin_send(shift).wait_send()


def gather_all(amplitudes, integrals, count_va, count_vb):
    occ_a, occ_b, row_len, col_len = amplitudes.shape
    blocks, rows, cols = integrals.shape
    chunks = blocks * SPLIT
    ratio = count_va // count_vb
    lines = count_va // PAIR
    outers = count_vb // PAIR
    flip = row_len % TILE == 0
    operands = (amplitudes, integrals)
    if not flip:
        turned = amplitudes.reshape(occ_a, occ_b, row_len, ratio, row_len)
        operands = (amplitudes, jnp.transpose(turned, (3, 0, 1, 4, 2)), integrals)
    mirror_shape = (ratio, occ_a, occ_b, row_len, row_len)
    dma = pltpu.SemaphoreType.DMA
    return pl.pallas_call(
        functools.partial(gather_kernel, count_va, count_vb, flip),
        out_shape=(
            jax.ShapeDtypeStruct((blocks, count_va * rows, cols), integrals.dtype),
            jax.ShapeDtypeStruct((count_vb, occ_a, occ_b, row_len, col_len), amplitudes.dtype),
        ),
        in_specs=[pl.BlockSpec(memory_space=pltpu.VMEM)] * (len(operands) - 1)
        + [pl.BlockSpec(memory_space=pl.ANY)],
        out_specs=(pl.BlockSpec(memory_space=pl.ANY),) * 2,
        scratch_shapes=[
            pltpu.VMEM(mirror_shape, amplitudes.dtype),
            pltpu.VMEM(mirror_shape, amplitudes.dtype),
            pltpu.VMEM(amplitudes.shape, amplitudes.dtype),
            dma((2, lines, chunks + 1)),
            dma((2, lines, chunks + 1)),
            dma((2, lines, chunks)),
            dma((2, lines, chunks)),
            dma((2, ratio, occ_a)),
            dma((ratio, occ_a)),
            dma((ratio, occ_a)),
            dma((ratio, occ_a)),
            dma((2, outers)),
            dma((2, outers)),
            dma((ratio + 1 + chunks,)),
        ],
        compiler_params=pltpu.CompilerParams(has_side_effects=True),
    )(*operands)


def cycle_kernel(at, screen, lengths, occ, *refs):
    spin_refs, k_refs = refs[:GROUP], refs[GROUP : 2 * GROUP]
    rows_ref, cols_ref, out_ref = refs[2 * GROUP :]
    slot = pl.program_id(0) * GROUP
    occ_count = out_ref.shape[0]
    count = lengths[at[0]]
    row_len = out_ref.shape[2]

    @pl.when(slot == 0)
    def _():
        out_ref[...] = jnp.zeros_like(out_ref)

    @pl.when(slot < count)
    def _():
        pairs = [(m, k) for m in range(GROUP) for k in range(occ_count)]
        live = [(slot + m < count).astype(spin_refs[0].dtype) for m in range(GROUP)]
        lefts = [
            jnp.concatenate([spin_refs[m][0, i, k] * live[m] for m, k in pairs], axis=1)
            for i in range(occ_count)
        ]
        for j in range(occ_count):
            right = jnp.concatenate([k_refs[m][k * occ_count + j] for m, k in pairs], axis=0)
            for i in range(occ_count):
                out_ref[i, j] += jnp.dot(lefts[i], right, preferred_element_type=jnp.float32)

    @pl.when(pl.program_id(0) == pl.num_programs(0) - 1)
    def _():
        vir_rows = jnp.broadcast_to(rows_ref[0], (TILE, row_len)).T[:, :1]
        for i in range(occ_count):
            for j in range(occ_count):
                bottom = (occ[i] + occ[j] - vir_rows) - cols_ref[0]
                out_ref[i, j] = out_ref[i, j] / bottom


GROUPS = 2
LATE = [(2, "out", 6), (2, "in", 4), (4, "out", 7), (4, "in", 5), (6, "in", 6), (8, "in", 7)]

OUT, IN_SIDE, IN_NEAR, IN_FAR, USE, MIRROR, LIVE, LEFT, PAIRS, ROWS = 0, 1, 2, 3, 4, 6, 8, 10, 12, 16


def bit_count(value):
    value = value - ((value >> 1) & 0x5555)
    value = (value & 0x3333) + ((value >> 2) & 0x3333)
    value = (value + (value >> 4)) & 0x0F0F
    return (value + (value >> 8)) & 0x1F


def power(place):
    result = 1 + place % 2
    for bit in range(1, 4):
        result = result * (1 + (2 ** 2**bit - 1) * (place // 2**bit % 2))
    return result


def bit_rank(mask, place):
    return bit_count(mask & (power(place) - 1))


def set_bits(mask, count, spare):
    places = []
    for _ in range(count):
        low = mask & -mask
        places.append(jnp.where(mask == 0, spare, bit_count(low - 1)))
        mask = mask & (mask - 1)
    return places


def row_masks(screen, lengths, count_va, slots):
    def one(m, masks):
        return tuple(
            mask | jnp.where(m < lengths[row], power(jnp.maximum(screen[row, m], 0)), 0) for row, mask in enumerate(masks)
        )

    return lax.fori_loop(0, slots, one, (jnp.int32(0),) * count_va)


def level_tiles(level, per_level):
    return ((1 << per_level) - 1) << (level * per_level)


def any_of(masks):
    return functools.reduce(lambda one, two: one | two, masks)


def link_masks(masks, levels, per_level):
    wanted = [any_of(masks[level * PAIR : (level + 1) * PAIR]) for level in range(levels)]
    half = levels // 2
    end_out, mid_out, end_in = [], [], []
    for side in range(2):
        end = 0 if side == 0 else levels - 1
        mine = range(half) if side == 0 else range(half, levels)
        end_tiles = level_tiles(end, per_level)
        end_out.append(end_tiles & any_of([wanted[l] for l in range(levels) if l != end]))
        mid_out.append(
            any_of([level_tiles(l, per_level) for l in mine]) & any_of([wanted[l] for l in range(levels) if l not in mine])
        )
        end_in.append(wanted[end] & ~end_tiles)
    return end_out, mid_out, end_in


def pair_mask(low, high, level, per_level):
    every = (1 << per_level) - 1
    return ((low >> (level * per_level)) & every) | (((high >> (level * per_level)) & every) << per_level)


def listed_kernel(caps, slots, table_ref, occ_ref, amp_ref, int_ref, rows_from, cols_from, out_ref, *refs):
    first_cap, mid_cap, end_cap, pair_cap = caps
    refs = list(refs)
    count_va = lax.axis_size("va")
    levels = count_va // PAIR
    occ_count = amp_ref.shape[0]
    own_tiles = int_ref.shape[1]
    rows = own_tiles * TILE
    cols = int_ref.shape[3]
    per_level = own_tiles * PAIR
    col_parts = cols // TILE
    units = occ_count * col_parts
    pairs = slots + slots // 2
    group = pairs // GROUPS

    near = [refs.pop(0) for _ in range(units)]
    far = [refs.pop(0) for _ in range(units)]
    out_pack = [refs.pop(0) for _ in range(units)]
    in_pack = [refs.pop(0) for _ in range(units)]
    share, sib, mirror_out, mirror_in, spin_mine, spin_other = [
        [refs.pop(0) for _ in range(PAIR)] for _ in range(6)
    ]
    (
        lefts, rights, vir_rows, part_own, part_out, part_in, table, occ, rows_ref, cols_ref, load_sem, near_sem, own_sem,
        y_send, y_recv, out_send, near_recv, far_recv, in_send, a_send, a_recv, sib_send, sib_recv, m_send, m_recv,
        x_send, x_recv, c_send, c_recv, p_send, p_recv,
    ) = refs

    va = lax.axis_index("va")
    vb = lax.axis_index("vb")
    z, y = va // PAIR, va % PAIR
    x, c = vb // PAIR, vb % PAIR
    upper = z // (levels // 2)
    inner = jnp.where(upper == 0, z, levels - 1 - z)
    toward = jnp.where(upper == 0, PAIR, -PAIR)
    end_level = jnp.where(upper == 0, 0, levels - 1)
    lead = z % PAIR
    own_at = per_level + y * own_tiles

    def remote(src, dst, send, recv, target):
        return pltpu.make_async_remote_copy(
            src_ref=src, dst_ref=dst, send_sem=send, recv_sem=recv, device_id=target, device_id_type=MESH
        )

    def tile_rows(begin):
        return pl.ds(pl.multiple_of(begin * TILE, TILE), TILE)

    def unit(u):
        return u // col_parts, pl.ds(u % col_parts * TILE, TILE)

    def y_copy(u):
        j, at = unit(u)
        return remote(
            int_ref.at[(1 - y) * occ_count + j, :, :, at], near[u].at[pl.ds(own_at, own_tiles)],
            y_send.at[u], y_recv.at[u], {"va": z * PAIR + 1 - y},
        )

    def y_arrival(u):
        here = near[u].at[pl.ds(per_level + (1 - y) * own_tiles, own_tiles)]
        return remote(here, here, y_send.at[u], y_recv.at[u], {"va": va})

    flips = [(1, 0), (0, 1), (1, 1)]

    def flipped(f):
        flip_x, flip_y = flips[f]
        return x + flip_x * (1 - 2 * x), y + flip_y * (1 - 2 * y)

    def block_tiles(at_x, at_y, side):
        return pl.ds(((at_x * PAIR + at_y) * PAIR + side) * own_tiles, own_tiles)

    def half_cols(side, half):
        return pl.ds((side * PAIR + half) * TILE, TILE)

    def share_copy(half, f, side):
        to_x, to_y = flipped(f)
        return remote(
            amp_ref.at[to_x, to_y, :, :, half_cols(side, half)], share[half].at[block_tiles(x, y, side)],
            a_send.at[half, f, side], a_recv.at[half, f, side], {"va": z * PAIR + to_y, "vb": to_x * PAIR + c},
        )

    def share_arrival(half, f, side):
        here = share[half].at[block_tiles(*flipped(f), side)]
        return remote(here, here, a_send.at[half, f, side], a_recv.at[half, f, side], {"va": va})

    def each_share(act):
        for f in range(3):
            for side in range(PAIR):
                act(f, side)

    loads = [
        pltpu.make_async_copy(src, dst, load_sem.at[n])
        for n, (src, dst) in enumerate(
            [
                (table_ref, table), (occ_ref, occ),
                (rows_from.at[va], rows_ref), (cols_from.at[vb], cols_ref),
            ]
        )
    ]

    def near_own(u):
        j, at = unit(u)
        return pltpu.make_async_copy(
            int_ref.at[y * occ_count + j, :, :, at], near[u].at[pl.ds(own_at, own_tiles)], near_sem.at[u]
        )

    def share_own(half, side):
        return pltpu.make_async_copy(
            amp_ref.at[x, y, :, :, half_cols(side, half)], share[half].at[block_tiles(x, y, side)], own_sem.at[half, side]
        )

    for load in loads:
        load.start()
    for u in range(units):
        near_own(u).start()
    for half in range(PAIR):
        for side in range(PAIR):
            share_own(half, side).start()

    barrier = pltpu.get_barrier_semaphore()
    partners = [{"vb": x * PAIR + 1 - c}]
    for f in range(3):
        to_x, to_y = flipped(f)
        partners.append({"va": z * PAIR + to_y, "vb": to_x * PAIR + c})
    for step in range(1, levels):
        partners.append({"va": lax.rem(z + step, levels) * PAIR + y})
    for partner in partners:
        pl.semaphore_signal(barrier, inc=1, device_id=partner, device_id_type=MESH)
    pl.semaphore_wait(barrier, len(partners))

    y_copy(0).start()
    each_share(lambda f, side: share_copy(0, f, side).start())

    for load in loads:
        load.wait()
    vir_rows[...] = jnp.broadcast_to(rows_ref[...], (TILE, rows)).T

    def out_copy(u, end):
        if end:
            here, there = out_pack[u].at[pl.ds(0, first_cap)], near[u].at[pl.ds(0, first_cap)]
            return remote(here, there, out_send.at[u], near_recv.at[u], {"va": va + toward})
        here, there = out_pack[u].at[pl.ds(0, mid_cap)], far[u].at[pl.ds(0, mid_cap)]
        return remote(here, there, out_send.at[u], far_recv.at[u], {"va": va + toward})

    def near_arrival(u):
        here = near[u].at[pl.ds(0, first_cap)]
        return remote(here, here, out_send.at[u], near_recv.at[u], {"va": va})

    def far_arrival(u, end):
        here = far[u].at[pl.ds(0, end_cap if end else mid_cap)]
        return remote(here, here, out_send.at[u], far_recv.at[u], {"va": va})

    def in_copy(u):
        here, there = in_pack[u].at[pl.ds(0, end_cap)], far[u].at[pl.ds(0, end_cap)]
        return remote(here, there, in_send.at[u], far_recv.at[u], {"va": va - toward})

    def out_step(u):
        near_own(u).wait()
        y_arrival(u).wait_recv()

        @pl.when(inner == 1)
        def _():
            near_arrival(u).wait_recv()

        @functools.partial(lax.fori_loop, 0, max(first_cap, mid_cap), init_val=0)
        def _(s, carry):
            out_pack[u][s] = near[u][table[OUT, s]]
            return carry

        @pl.when(inner == 0)
        def _():
            out_copy(u, True).start()

        @pl.when(inner == 1)
        def _():
            out_copy(u, False).start()

    def in_step(u):
        @pl.when(inner == 1)
        def _():
            far_arrival(u, False).wait_recv()

            @functools.partial(lax.fori_loop, 0, end_cap, init_val=0)
            def _(s, carry):
                in_pack[u][s] = jnp.where(
                    table[IN_SIDE, s] == 1, near[u][table[IN_NEAR, s]], far[u][table[IN_FAR, s]]
                )
                return carry

            in_copy(u).start()

    def sib_copy(half):
        return remote(share[half], sib[half], sib_send.at[half], sib_recv.at[half], {"vb": x * PAIR + 1 - c})

    def sib_arrival(half):
        return remote(sib[half], sib[half], sib_send.at[half], sib_recv.at[half], {"vb": vb})

    def mirror_copy(half, at_x):
        level = at_x * PAIR + c
        return remote(
            mirror_out[half].at[pl.ds(at_x * pair_cap, pair_cap)],
            mirror_in[half].at[pl.ds(z * pair_cap, pair_cap)],
            m_send.at[half, at_x], m_recv.at[half, z], {"va": level * PAIR + y},
        )

    def mirror_arrival(half, level):
        here = mirror_in[half].at[pl.ds(level * pair_cap, pair_cap)]
        return remote(here, here, m_send.at[half, 0], m_recv.at[half, level], {"va": va})

    def share_step(half):
        each_share(lambda f, side: share_arrival(half, f, side).wait_recv())
        for side in range(PAIR):
            share_own(half, side).wait()
        for at_x in range(PAIR):
            level = at_x * PAIR + c

            @functools.partial(lax.fori_loop, 0, pair_cap, init_val=0)
            def _(s, carry):
                place = table[MIRROR + at_x, s]
                side, tile = place // per_level, place % per_level
                block = (at_x * PAIR + tile // own_tiles) * PAIR + side
                mirror_out[half][at_x * pair_cap + s] = share[half][block * own_tiles + tile % own_tiles]
                return carry

            @pl.when(level != z)
            def _():
                mirror_copy(half, at_x).start()

            @pl.when(level == z)
            def _():
                mirror_in[half][pl.ds(z * pair_cap, pair_cap)] = mirror_out[half][
                    pl.ds(at_x * pair_cap, pair_cap)
                ]

        @pl.when(c != lead)
        def _():
            sib_copy(half).start()

    def spin_group(ref, g):
        return ref.at[pl.ds(g * group, group)]

    def x_copy(half, g):
        return remote(
            spin_group(spin_mine[half], g), spin_group(spin_other[half], g), x_send.at[half, g], x_recv.at[half, g],
            {"vb": (1 - x) * PAIR + c},
        )

    def x_arrival(half, g):
        here = spin_group(spin_other[half], g)
        return remote(here, here, x_send.at[half, g], x_recv.at[half, g], {"vb": vb})

    def core_copy(which, half, g):
        ref = (spin_mine, spin_other)[which][half]
        return remote(
            spin_group(ref, g), spin_group(ref, g), c_send.at[which, half, g], c_recv.at[which, half, g],
            {"vb": x * PAIR + 1 - c},
        )

    def core_arrival(which, half, g):
        here = spin_group((spin_mine, spin_other)[which][half], g)
        return remote(here, here, c_send.at[which, half, g], c_recv.at[which, half, g], {"vb": vb})

    def spin_step(half):
        @pl.when(c == lead)
        def _():
            for level in range(levels):

                @pl.when(level != z)
                def _():
                    mirror_arrival(half, level).wait_recv()

            if half == 0:
                for one in range(PAIR):
                    sib_arrival(one).wait_recv()
            for g in range(GROUPS):

                @functools.partial(lax.fori_loop, g * group, (g + 1) * group, init_val=0)
                def _(q, carry):
                    side, tile, place = table[PAIRS, q], table[PAIRS + 1, q], table[PAIRS + 2, q] * pair_cap + table[PAIRS + 3, q]
                    owner, within = tile // col_parts, tile % col_parts
                    block = ((owner // PAIR) * PAIR + side) * PAIR + within // PAIR
                    at = block * own_tiles + half
                    first, second = [
                        jnp.where(owner % PAIR == lead, share[one][at], sib[one][at]) for one in range(PAIR)
                    ]
                    own = jnp.where(within % PAIR == 0, first, second)
                    mirror = mirror_in[half][place]
                    spin = 2.0 * own.astype(jnp.float32) - mirror.astype(jnp.float32).T
                    spin_mine[half][q] = spin.astype(amp_ref.dtype)
                    return carry

                x_copy(half, g).start()
                core_copy(0, half, g).start()

    def pass_step(half):
        @pl.when(c == lead)
        def _():
            for g in range(GROUPS):
                x_arrival(half, g).wait_recv()
                core_copy(1, half, g).start()

    def left_step(half):
        @pl.when(c != lead)
        def _():
            for g in range(GROUPS):
                for which in range(2):
                    core_arrival(which, half, g).wait_recv()

        @functools.partial(lax.fori_loop, 0, PAIR * slots, init_val=0)
        def _(index, carry):
            side, m = index // slots, index % slots
            live = table[LIVE + side, m] == 1
            q = table[LEFT + side, m]
            lanes = pl.ds(pl.multiple_of(m * TILE, TILE), TILE)
            for ref, place in ((spin_mine, x), (spin_other, 1 - x)):
                value = ref[half][q]
                lefts[half, side, tile_rows(place), lanes] = jnp.where(live, value, jnp.zeros_like(value))
            return carry

    def part_copy(u, half):
        return remote(
            part_out.at[u, half], part_in.at[u, half], p_send.at[u, half], p_recv.at[u, half], {"va": z * PAIR + 1 - y}
        )

    def part_arrival(u, half):
        return remote(part_in.at[u, half], part_in.at[u, half], p_send.at[u, half], p_recv.at[u, half], {"va": va})

    def end_wait(u):
        @pl.when(inner == 0)
        def _():
            far_arrival(u, True).wait_recv()

    def gather_step(u):
        @functools.partial(lax.fori_loop, 0, PAIR * slots, init_val=0)
        def _(index, carry):
            side, m = index // slots, index % slots
            place = table[USE + side, m]
            here = jnp.minimum(place, 2 * per_level - 1)
            there = jnp.maximum(place - 2 * per_level, 0)
            rights[u, side, tile_rows(m), :] = jnp.where(place < 2 * per_level, near[u][here], far[u][there])
            return carry

    def dot_step(u, half):
        total = jnp.dot(lefts[half, 1 - y], rights[u, 1 - y], preferred_element_type=jnp.float32)
        part_out[u, half] = total.astype(part_out.dtype)
        part_copy(u, half).start()
        part_own[u, half] = jnp.dot(lefts[half, y], rights[u, y], preferred_element_type=jnp.float32)

    def final_step(u, half):
        j = u // col_parts
        at = pl.ds(pl.multiple_of(u % col_parts * TILE, TILE), TILE)
        part_arrival(u, half).wait_recv()
        part_rows = tile_rows(half)
        for i in range(occ_count):
            bottom = (occ[i] + occ[j] - vir_rows[part_rows, :]) - cols_ref[:, at]
            here = pl.ds(i * TILE, TILE)
            whole = part_own[u, half, here, :] + part_in[u, half, here, :].astype(jnp.float32)
            out_ref[i, j, part_rows, at] = whole / bottom

    def y_start(u):
        if u < units:
            y_copy(u).start()

    out_step(0)
    y_start(1)
    each_share(lambda f, side: share_copy(1, f, side).start())
    share_step(0)
    y_start(2)
    out_step(1)
    y_start(3)
    share_step(1)
    in_step(0)
    out_step(2)
    y_start(4)
    in_step(1)
    out_step(3)
    y_start(5)
    spin_step(0)
    in_step(2)
    out_step(4)
    y_start(6)
    pass_step(0)
    spin_step(1)
    y_start(7)
    in_step(3)
    out_step(5)
    left_step(0)

    stages = units * PAIR
    early = units // 2
    actions = {stage: [] for stage in range(stages)}
    for u in range(units):
        stage = u if u < early else early * PAIR + (u - early) * PAIR
        actions[stage] += [functools.partial(end_wait, u), functools.partial(gather_step, u)]
    actions[early] = [functools.partial(pass_step, 1), functools.partial(left_step, 1), *actions[early]]
    for stage, step, u in LATE:
        actions[stage] = [functools.partial({"in": in_step, "out": out_step}[step], u), *actions[stage]]

    @functools.partial(lax.fori_loop, 0, stages, init_val=0)
    def _(stage, carry):
        for at, acts in actions.items():
            if acts:

                @pl.when(stage == at)
                def _():
                    for act in acts:
                        act()

        first = stage < early * PAIR
        u = jnp.where(first, stage % early, stage // PAIR)
        dot_step(u, jnp.where(first, stage // early, stage % PAIR))
        return carry

    @functools.partial(lax.fori_loop, 0, stages, init_val=0)
    def _(stage, carry):
        first = stage < early * PAIR
        u = jnp.where(first, stage % early, stage // PAIR)
        final_step(u, jnp.where(first, stage // early, stage % PAIR))
        return carry

    for u in range(units):
        y_copy(u).wait_send()
        for half in range(PAIR):
            part_copy(u, half).wait_send()

        @pl.when(inner == 0)
        def _():
            out_copy(u, True).wait_send()

        @pl.when(inner == 1)
        def _():
            out_copy(u, False).wait_send()
            in_copy(u).wait_send()

    for half in range(PAIR):
        each_share(lambda f, side: share_copy(half, f, side).wait_send())
        for at_x in range(PAIR):

            @pl.when(at_x * PAIR + c != z)
            def _():
                mirror_copy(half, at_x).wait_send()

        @pl.when(c != lead)
        def _():
            sib_copy(half).wait_send()

        @pl.when(c == lead)
        def _():
            for g in range(GROUPS):
                x_copy(half, g).wait_send()
                for which in range(2):
                    core_copy(which, half, g).wait_send()


def listed_all(index, caps, slots, amplitudes, integrals, occ_energy, vir_energy, table):
    first_cap, mid_cap, end_cap, pair_cap = caps
    count_va = lax.axis_size("va")
    count_vb = lax.axis_size("vb")
    occ_a, occ_b, row_len, col_len = amplitudes.shape
    blocks, rows, cols = integrals.shape
    levels = count_va // PAIR
    own_tiles = rows // TILE
    per_level = own_tiles * PAIR
    units = occ_a * (cols // TILE)
    pairs = slots + slots // 2
    kind = amplitudes.dtype
    dma = pltpu.SemaphoreType.DMA
    vmem = pltpu.VMEM
    return pl.pallas_call(
        functools.partial(listed_kernel, caps, slots),
        out_shape=jax.ShapeDtypeStruct((occ_a, occ_b, row_len, cols), jnp.float32),
        in_specs=[pl.BlockSpec(memory_space=pl.ANY)] * 6,
        out_specs=pl.BlockSpec(memory_space=vmem),
        scratch_shapes=[
            *[vmem((2 * per_level, TILE, TILE), kind)] * units,
            *[vmem((max(mid_cap, end_cap), TILE, TILE), kind)] * units,
            *[vmem((max(first_cap, mid_cap), TILE, TILE), kind)] * units,
            *[vmem((end_cap, TILE, TILE), kind)] * units,
            *[vmem((PAIR * PAIR * PAIR * own_tiles, TILE, TILE), kind)] * (2 * PAIR),
            *[vmem((PAIR * pair_cap, TILE, TILE), kind)] * PAIR,
            *[vmem((levels * pair_cap, TILE, TILE), kind)] * PAIR,
            *[vmem((pairs, TILE, TILE), kind)] * (2 * PAIR),
            vmem((PAIR, PAIR, occ_a * TILE, slots * TILE), kind),
            vmem((units, PAIR, slots * TILE, TILE), kind),
            vmem((rows, TILE), jnp.float32),
            vmem((units, PAIR, occ_a * TILE, TILE), jnp.float32),
            vmem((units, PAIR, occ_a * TILE, TILE), kind),
            vmem((units, PAIR, occ_a * TILE, TILE), kind),
            pltpu.SMEM(table.shape, table.dtype),
            pltpu.SMEM(occ_energy.shape, occ_energy.dtype),
            vmem((1, row_len), jnp.float32),
            vmem((1, cols), jnp.float32),
            dma((4,)),
            dma((units,)),
            dma((PAIR, PAIR)),
            *[dma((units,))] * 6,
            *[dma((PAIR, 3, PAIR))] * 2,
            *[dma((PAIR,))] * 2,
            dma((PAIR, PAIR)), dma((PAIR, levels)),
            *[dma((PAIR, GROUPS))] * 2,
            *[dma((2, PAIR, GROUPS))] * 2,
            *[dma((units, PAIR))] * 2,
        ],
        compiler_params=pltpu.CompilerParams(collective_id=index, has_side_effects=True, vmem_limit_bytes=60 * 2**20),
    )(
        table, occ_energy, amplitudes.reshape(occ_a, occ_b, own_tiles, TILE, col_len),
        integrals.reshape(blocks, own_tiles, TILE, cols),
        vir_energy.reshape(count_va, 1, row_len), vir_energy.reshape(count_vb, 1, cols),
    )


def fits(amplitudes, integrals, screen, count_va, count_vb):
    levels = count_va // PAIR
    rows, cols = integrals.shape[1:]
    return (
        levels == PAIR * PAIR
        and count_vb == levels
        and amplitudes.shape[0] == PAIR
        and rows == PAIR * TILE
        and cols == PAIR * rows
        and count_va * rows == ROWS * TILE
        and screen.shape[1] % 4 == 0
    )


def dense(amplitudes, integrals, occ_energy, vir_energy, screen, lengths):
    count_va = lax.axis_size("va")
    count_vb = lax.axis_size("vb")
    occ_a, occ_b, row_len, col_len = amplitudes.shape
    cols = integrals.shape[2]
    whole_k, spin_all = gather_all(amplitudes, integrals, count_va, count_vb)
    slots = screen.shape[1]
    per_shard = col_len // TILE
    at = jnp.stack([lax.axis_index("va"), lax.axis_index("vb")]).astype(jnp.int32)

    def tile_of(m, at, screen, lengths):
        return jnp.maximum(screen[at[0], jnp.minimum(m, lengths[at[0]] - 1)], 0)

    def spin_at(place, m, at, screen, lengths, occ):
        tile = tile_of(m * GROUP + place, at, screen, lengths)
        return (tile // per_shard, 0, 0, 0, tile % per_shard)

    def k_at(place, m, at, screen, lengths, occ):
        return (0, tile_of(m * GROUP + place, at, screen, lengths), 0)

    return pl.pallas_call(
        cycle_kernel,
        out_shape=jax.ShapeDtypeStruct((occ_a, occ_b, row_len, cols), jnp.float32),
        grid_spec=pltpu.PrefetchScalarGridSpec(
            num_scalar_prefetch=4,
            grid=(pl.cdiv(slots, GROUP),),
            in_specs=[
                *(
                    pl.BlockSpec((1, occ_a, occ_b, row_len, TILE), functools.partial(spin_at, place))
                    for place in range(GROUP)
                ),
                *(
                    pl.BlockSpec((integrals.shape[0], TILE, cols), functools.partial(k_at, place))
                    for place in range(GROUP)
                ),
                pl.BlockSpec((1, 1, row_len), lambda m, at, screen, lengths, occ: (at[0], 0, 0)),
                pl.BlockSpec((1, 1, cols), lambda m, at, screen, lengths, occ: (at[1], 0, 0)),
            ],
            out_specs=pl.BlockSpec(
                (occ_a, occ_b, row_len, cols), lambda m, at, screen, lengths, occ: (0, 0, 0, 0)
            ),
        ),
    )(
        at, screen, lengths, occ_energy, *[spin_all] * GROUP, *[whole_k] * GROUP,
        vir_energy.reshape(count_va, 1, row_len), vir_energy.reshape(count_vb, 1, cols),
    )


CAPS = ((4, 6, 6, 5), (4, 7, 8, 6), (4, 8, 12, 8))


def plan_kernel(caps, per_level, screen_ref, lengths_ref, choice, table, screen, lengths, load_sem):
    loads = [
        pltpu.make_async_copy(src, dst, load_sem.at[n])
        for n, (src, dst) in enumerate([(screen_ref, screen), (lengths_ref, lengths)])
    ]
    for load in loads:
        load.start()
    for load in loads:
        load.wait()
    count_va, slots = screen.shape
    levels = count_va // PAIR
    tiles = levels * per_level
    pairs = slots + slots // 2
    z = lax.axis_index("va") // PAIR
    c = lax.axis_index("vb") % PAIR
    upper = z // (levels // 2)
    inner = jnp.where(upper == 0, z, levels - 1 - z)
    end_level = jnp.where(upper == 0, 0, levels - 1)

    masks = row_masks(screen, lengths, count_va, slots)
    end_out, mid_out, end_in = [
        (jnp.where(upper == 0, one[0], one[1]), jnp.where(upper == 0, one[1], one[0]))
        for one in link_masks(masks, levels, per_level)
    ]

    def near_place(tile):
        level = tile // per_level
        from_end = jnp.logical_and(inner == 1, level == end_level)
        is_near = jnp.logical_or(level == z, from_end)
        place = jnp.where(level == z, per_level + tile % per_level, jnp.where(from_end, bit_rank(end_out[0], tile), per_level))
        return is_near, jnp.minimum(place, 2 * per_level - 1)

    def far_place(tile):
        return jnp.where(inner == 1, bit_rank(mid_out[1], tile), bit_rank(end_in[0], tile))

    spare = z * per_level
    for s, tile in enumerate(set_bits(jnp.where(inner == 1, mid_out[0], end_out[0]), per_level * PAIR, spare)):
        table[OUT, s] = near_place(tile)[1]
    for s, tile in enumerate(set_bits(end_in[0], tiles - per_level, spare)):
        is_near, place = near_place(tile)
        table[IN_SIDE, s] = is_near.astype(jnp.int32)
        table[IN_NEAR, s] = place
        table[IN_FAR, s] = far_place(tile)

    def of_level(level, side):
        mask = masks[side]
        for l in range(1, levels):
            mask = jnp.where(level == l, masks[l * PAIR + side], mask)
        return mask

    for at_x in range(PAIR):
        level = at_x * PAIR + c
        mask = pair_mask(of_level(level, 0), of_level(level, 1), z, per_level)
        for s, place in enumerate(set_bits(mask, per_level * PAIR, 0)):
            table[MIRROR + at_x, s] = place

    own_masks = [of_level(z, side) for side in range(PAIR)]
    counts = [lengths[z * PAIR + side] for side in range(PAIR)]

    def own_count(side):
        return jnp.where(side == 0, counts[0], counts[1])

    @functools.partial(lax.fori_loop, 0, pairs, init_val=0)
    def _(q, carry):
        side = (q >= counts[0]).astype(jnp.int32)
        m = jnp.clip(jnp.where(side == 0, q, q - counts[0]), 0, slots - 1)
        tile = jnp.maximum(screen[z * PAIR + side, m], 0)
        level = tile // per_level
        mask = 0
        for l in range(levels):
            mask = jnp.where(level == l, pair_mask(own_masks[0], own_masks[1], l, per_level), mask)
        rank = bit_rank(mask, side * per_level + tile % per_level)
        table[PAIRS, q] = side
        table[PAIRS + 1, q] = tile
        table[PAIRS + 2, q] = level
        table[PAIRS + 3, q] = rank
        return carry

    @functools.partial(lax.fori_loop, 0, PAIR * slots, init_val=0)
    def _(index, carry):
        side, m = index // slots, index % slots
        tile = jnp.maximum(screen[z * PAIR + side, jnp.clip(own_count(side) - 1, 0, m)], 0)
        is_near, place = near_place(tile)
        table[USE + side, m] = jnp.where(is_near, place, 2 * per_level + far_place(tile))
        table[LIVE + side, m] = (m < own_count(side)).astype(jnp.int32)
        table[LEFT + side, m] = jnp.minimum(jnp.where(side == 0, m, counts[0] + m), pairs - 1)
        return carry

    middle = jnp.maximum(*map(bit_count, mid_out))
    ends = jnp.maximum(*map(bit_count, end_in))
    most = functools.reduce(
        jnp.maximum,
        [
            bit_count(pair_mask(masks[PAIR * to], masks[PAIR * to + 1], level, per_level))
            for to in range(levels)
            for level in range(levels)
        ],
    )
    chosen = jnp.int32(len(caps) - 1)
    for index, (_, mid_cap, end_cap, pair_cap) in reversed(list(enumerate(caps[:-1]))):
        enough = jnp.logical_and(jnp.logical_and(middle <= mid_cap, ends <= end_cap), most <= pair_cap)
        chosen = jnp.where(enough, index, chosen)
    choice[0] = chosen


def plan(screen, lengths, per_level):
    return pl.pallas_call(
        functools.partial(plan_kernel, CAPS, per_level),
        out_shape=(jax.ShapeDtypeStruct((1,), jnp.int32), jax.ShapeDtypeStruct((ROWS, ROWS), jnp.int32)),
        in_specs=[pl.BlockSpec(memory_space=pl.ANY)] * 2,
        out_specs=(pl.BlockSpec(memory_space=pltpu.SMEM),) * 2,
        scratch_shapes=[
            pltpu.SMEM(screen.shape, screen.dtype),
            pltpu.SMEM(lengths.shape, lengths.dtype),
            pltpu.SemaphoreType.DMA((2,)),
        ],
        compiler_params=pltpu.CompilerParams(vmem_limit_bytes=60 * 2**20),
    )(screen, lengths)


def local(amplitudes, integrals, occ_energy, vir_energy, screen, lengths):
    operands = (amplitudes, integrals, occ_energy, vir_energy, screen, lengths)
    if not fits(amplitudes, integrals, screen, lax.axis_size("va"), lax.axis_size("vb")):
        return dense(*operands)
    choice, table = plan(screen, lengths, integrals.shape[1] // TILE * PAIR)
    branches = [functools.partial(listed_all, index, caps, screen.shape[1]) for index, caps in enumerate(CAPS)]
    return lax.switch(choice[0], branches, amplitudes, integrals, occ_energy, vir_energy, table)


def solution(mesh):
    return jax.shard_map(
        local,
        mesh=mesh,
        in_specs=(P(None, None, "va", "vb"), P(None, "va", "vb"), P(), P(), P(), P()),
        out_specs=P(None, None, "va", "vb"),
        check_vma=False,
    )
```

```python
import functools

import jax
import jax.numpy as jnp
from jax import lax
from jax.experimental import pallas as pl
from jax.experimental.pallas import tpu as pltpu
from jax.sharding import PartitionSpec as P

TILE = 128
PAIR = 2
SPLIT = 2
GROUP = 2
MESH = pl.DeviceIdType.MESH


def gather_kernel(
    count_va, count_vb, flip, amp_ref, *refs
):
    refs = list(refs)
    turned_ref = None if flip else refs.pop(0)
    (
        int_ref, whole_k, spin_all,
        landed, passing, spin, z_send, z_recv, y_send, y_recv, m_send, m_recv, x_send, x_recv, s_send, s_recv, own_sem,
    ) = refs
    va = lax.axis_index("va")
    vb = lax.axis_index("vb")
    ratio = count_va // count_vb
    lines = count_va // PAIR
    outers = count_vb // PAIR
    line, side = va // PAIR, va % PAIR
    outer, core = vb // PAIR, vb % PAIR
    blocks, rows, _ = int_ref.shape
    part_rows = rows // SPLIT
    chunks = blocks * SPLIT
    early = chunks - 1
    halves = amp_ref.shape[0]
    row_len = amp_ref.shape[2]

    def k_slot(owner, chunk):
        begin = owner * rows + chunk % SPLIT * part_rows
        return whole_k.at[chunk // SPLIT, pl.ds(pl.multiple_of(begin, part_rows), part_rows)]

    def own_slot(chunk):
        return int_ref.at[chunk // SPLIT, pl.ds(chunk % SPLIT * part_rows, part_rows)]

    def remote(src, dst, send, recv, target):
        return pltpu.make_async_remote_copy(
            src_ref=src, dst_ref=dst, send_sem=send, recv_sem=recv, device_id=target, device_id_type=MESH
        )

    next_vb = lax.rem(outer + 1, outers) * PAIR + core
    last_vb = lax.rem(outer + outers - 1, outers) * PAIR + core

    def by_relay(half):
        return outers > 1 and half % 2 == 1

    def piece(part):
        if flip:
            return amp_ref.at[:, :, :, pl.ds(part * row_len, row_len)]
        return turned_ref.at[part]

    def half_piece(part, half):
        if flip:
            return amp_ref.at[half, :, :, pl.ds(part * row_len, row_len)]
        return turned_ref.at[part, half]

    def mirror_own(part):
        return pltpu.make_async_copy(piece(part), landed.at[part], own_sem.at[part])

    def mirror_straight(part, half):
        return remote(
            half_piece(part, half), landed.at[va % ratio, half],
            m_send.at[0, part, half], m_recv.at[va % ratio, half],
            {"va": vb * ratio + part, "vb": va // ratio},
        )

    def mirror_out(part, half):
        return remote(
            half_piece(part, half), passing.at[part, half],
            x_send.at[part, half], x_recv.at[part, half], {"vb": next_vb},
        )

    def mirror_on(part, half):
        return remote(
            passing.at[part, half], landed.at[va % ratio, half],
            m_send.at[1, part, half], m_recv.at[va % ratio, half],
            {"va": last_vb * ratio + part, "vb": va // ratio},
        )

    def mirror_passing(part, half):
        here = passing.at[part, half]
        return remote(here, here, x_send.at[part, half], x_recv.at[part, half], {"vb": vb})

    def mirror_arrival(part, half):
        here = landed.at[part, half]
        return remote(here, here, m_send.at[0, part, half], m_recv.at[part, half], {"vb": vb})

    def stays(part):
        return va == vb * ratio + part

    def last_stays(part):
        return va == last_vb * ratio + part

    def each_mirror(own, straight, out):
        for part in range(ratio):

            @pl.when(stays(part))
            def _():
                own(part)

            @pl.when(jnp.logical_not(stays(part)))
            def _():
                for half in range(halves):
                    (out if by_relay(half) else straight)(part, half)

    each_mirror(
        lambda part: mirror_own(part).start(),
        lambda part, half: mirror_straight(part, half).start(),
        lambda part, half: mirror_out(part, half).start(),
    )

    def each_passing(act):
        for part in range(ratio):

            @pl.when(jnp.logical_not(last_stays(part)))
            def _():
                for half in range(halves):
                    if by_relay(half):
                        act(part, half)

    def source(direction, step):
        return line - step if direction == 0 else line + step

    def line_slot(direction, step, chunk):
        if chunk == chunks:
            return k_slot(source(direction, step) * PAIR + 1 - side, early)
        return k_slot(source(direction, step) * PAIR + side, chunk)

    def block_at(direction, step, chunk):
        if step == 0 and chunk < chunks:
            return own_slot(chunk)
        return line_slot(direction, step, chunk)

    def line_send(direction, step, chunk):
        to = line + 1 if direction == 0 else line - 1
        return remote(
            block_at(direction, step, chunk),
            line_slot(direction, step, chunk),
            z_send.at[direction, step, chunk],
            z_recv.at[direction, step, chunk],
            {"va": to * PAIR + side},
        )

    def line_arrival(direction, step, chunk):
        here = line_slot(direction, step, chunk)
        return remote(
            here, here, z_send.at[direction, step - 1, chunk], z_recv.at[direction, step - 1, chunk],
            {"va": va},
        )

    def may_send(direction, step):
        if direction == 0:
            return jnp.logical_and(line - step >= 0, line + 1 < lines)
        return jnp.logical_and(line + step < lines, line - 1 >= 0)

    def has_arrival(direction, step):
        return line - step >= 0 if direction == 0 else line + step < lines

    def side_send(direction, step, chunk):
        return remote(
            block_at(direction, step, chunk),
            line_slot(direction, step, chunk),
            y_send.at[direction, step, chunk],
            y_recv.at[direction, step, chunk],
            {"va": line * PAIR + 1 - side},
        )

    def side_arrival(direction, step, chunk):
        here = k_slot(source(direction, step) * PAIR + 1 - side, chunk)
        return remote(
            here, here, y_send.at[direction, step, chunk], y_recv.at[direction, step, chunk], {"va": va}
        )

    def own_copy(chunk):
        return pltpu.make_async_copy(own_slot(chunk), k_slot(va, chunk), own_sem.at[ratio + 1 + chunk])

    def send_own(chunk):
        for direction in range(2):

            @pl.when(may_send(direction, 0))
            def _():
                line_send(direction, 0, chunk).start()

    side_send(0, 0, early).start()
    for chunk in range(chunks):
        send_own(chunk)
        if chunk != early:
            side_send(0, 0, chunk).start()
    for chunk in range(chunks):
        own_copy(chunk).start()
    side_arrival(0, 0, early).wait_recv()
    send_own(chunks)

    def pass_mirror(part, half):
        mirror_passing(part, half).wait_recv()
        mirror_on(part, half).start()

    each_passing(pass_mirror)

    def line_step(step):
        for chunk in range(chunks + 1):
            for direction in range(2):

                @pl.when(has_arrival(direction, step))
                def _():
                    line_arrival(direction, step, chunk).wait_recv()

                    @pl.when(may_send(direction, step))
                    def _():
                        line_send(direction, step, chunk).start()

                    if chunk < early:
                        side_send(direction, step, chunk).start()

    def spin_send(shift):
        to = lax.rem(outer + shift, outers)
        return remote(
            spin, spin_all.at[vb], s_send.at[0, shift], s_recv.at[0, shift], {"vb": to * PAIR + core}
        )

    def spin_arrival(shift):
        here = spin_all.at[lax.rem(outer + outers - shift, outers) * PAIR + core]
        return remote(here, here, s_send.at[0, shift], s_recv.at[0, shift], {"vb": vb})

    def spin_relay(shift):
        held = spin_all.at[lax.rem(outer + outers - shift, outers) * PAIR + core]
        src = spin if shift == 0 else held
        return remote(
            src, held, s_send.at[1, shift], s_recv.at[1, shift], {"vb": outer * PAIR + 1 - core}
        )

    def relay_arrival(shift):
        here = spin_all.at[lax.rem(outer + outers - shift, outers) * PAIR + 1 - core]
        return remote(here, here, s_send.at[1, shift], s_recv.at[1, shift], {"vb": vb})

    def spin_own():
        return pltpu.make_async_copy(spin, spin_all.at[vb], own_sem.at[ratio])

    def spin_step():
        for part in range(ratio):

            @pl.when(stays(part))
            def _():
                mirror_own(part).wait()

            @pl.when(jnp.logical_not(stays(part)))
            def _():
                for half in range(halves):
                    mirror_arrival(part, half).wait_recv()

            cols = slice(part * row_len, (part + 1) * row_len)
            for i in range(halves):
                for k in range(amp_ref.shape[1]):
                    mirror = landed[part, i, k].astype(jnp.float32)
                    spin[i, k, :, cols] = (
                        2.0 * amp_ref[i, k, :, cols].astype(jnp.float32) - (mirror.T if flip else mirror)
                    ).astype(spin.dtype)
        for shift in range(1, outers):
            spin_send(shift).start()
        spin_relay(0).start()
        spin_own().start()

    spin_after = 1
    for step in range(1, lines):
        line_step(step)
        if step == spin_after:
            spin_step()
    if spin_after == 0:
        spin_step()
    for shift in range(1, outers):
        spin_arrival(shift).wait_recv()
        spin_relay(shift).start()

    for chunk in range(chunks + 1):
        if chunk < chunks:
            own_copy(chunk).wait()
            side_send(0, 0, chunk).wait_send()
            if chunk != early:
                side_arrival(0, 0, chunk).wait_recv()
        for direction in range(2):

            @pl.when(may_send(direction, 0))
            def _():
                line_send(direction, 0, chunk).wait_send()

    for step in range(1, lines):
        for chunk in range(chunks + 1):
            for direction in range(2):

                @pl.when(may_send(direction, step))
                def _():
                    line_send(direction, step, chunk).wait_send()

                if chunk < early:

                    @pl.when(has_arrival(direction, step))
                    def _():
                        side_arrival(direction, step, chunk).wait_recv()
                        side_send(direction, step, chunk).wait_send()

    each_mirror(
        lambda part: None,
        lambda part, half: mirror_straight(part, half).wait_send(),
        lambda part, half: mirror_out(part, half).wait_send(),
    )
    each_passing(lambda part, half: mirror_on(part, half).wait_send())

    spin_own().wait()
    for shift in range(outers):
        relay_arrival(shift).wait_recv()
        spin_relay(shift).wait_send()
    for shift in range(1, outers):
        spin_send(shift).wait_send()


def gather_all(amplitudes, integrals, count_va, count_vb):
    occ_a, occ_b, row_len, col_len = amplitudes.shape
    blocks, rows, cols = integrals.shape
    chunks = blocks * SPLIT
    ratio = count_va // count_vb
    lines = count_va // PAIR
    outers = count_vb // PAIR
    flip = row_len % TILE == 0
    operands = (amplitudes, integrals)
    if not flip:
        turned = amplitudes.reshape(occ_a, occ_b, row_len, ratio, row_len)
        operands = (amplitudes, jnp.transpose(turned, (3, 0, 1, 4, 2)), integrals)
    mirror_shape = (ratio, occ_a, occ_b, row_len, row_len)
    dma = pltpu.SemaphoreType.DMA
    return pl.pallas_call(
        functools.partial(gather_kernel, count_va, count_vb, flip),
        out_shape=(
            jax.ShapeDtypeStruct((blocks, count_va * rows, cols), integrals.dtype),
            jax.ShapeDtypeStruct((count_vb, occ_a, occ_b, row_len, col_len), amplitudes.dtype),
        ),
        in_specs=[pl.BlockSpec(memory_space=pltpu.VMEM)] * (len(operands) - 1)
        + [pl.BlockSpec(memory_space=pl.ANY)],
        out_specs=(pl.BlockSpec(memory_space=pl.ANY),) * 2,
        scratch_shapes=[
            pltpu.VMEM(mirror_shape, amplitudes.dtype),
            pltpu.VMEM(mirror_shape, amplitudes.dtype),
            pltpu.VMEM(amplitudes.shape, amplitudes.dtype),
            dma((2, lines, chunks + 1)),
            dma((2, lines, chunks + 1)),
            dma((2, lines, chunks)),
            dma((2, lines, chunks)),
            dma((2, ratio, occ_a)),
            dma((ratio, occ_a)),
            dma((ratio, occ_a)),
            dma((ratio, occ_a)),
            dma((2, outers)),
            dma((2, outers)),
            dma((ratio + 1 + chunks,)),
        ],
        compiler_params=pltpu.CompilerParams(has_side_effects=True),
    )(*operands)


def cycle_kernel(at, screen, lengths, occ, *refs):
    spin_refs, k_refs = refs[:GROUP], refs[GROUP : 2 * GROUP]
    rows_ref, cols_ref, out_ref = refs[2 * GROUP :]
    slot = pl.program_id(0) * GROUP
    occ_count = out_ref.shape[0]
    count = lengths[at[0]]
    row_len = out_ref.shape[2]

    @pl.when(slot == 0)
    def _():
        out_ref[...] = jnp.zeros_like(out_ref)

    @pl.when(slot < count)
    def _():
        pairs = [(m, k) for m in range(GROUP) for k in range(occ_count)]
        live = [(slot + m < count).astype(spin_refs[0].dtype) for m in range(GROUP)]
        lefts = [
            jnp.concatenate([spin_refs[m][0, i, k] * live[m] for m, k in pairs], axis=1)
            for i in range(occ_count)
        ]
        for j in range(occ_count):
            right = jnp.concatenate([k_refs[m][k * occ_count + j] for m, k in pairs], axis=0)
            for i in range(occ_count):
                out_ref[i, j] += jnp.dot(lefts[i], right, preferred_element_type=jnp.float32)

    @pl.when(pl.program_id(0) == pl.num_programs(0) - 1)
    def _():
        vir_rows = jnp.broadcast_to(rows_ref[0], (TILE, row_len)).T[:, :1]
        for i in range(occ_count):
            for j in range(occ_count):
                bottom = (occ[i] + occ[j] - vir_rows) - cols_ref[0]
                out_ref[i, j] = out_ref[i, j] / bottom


GROUPS = 2
LAG = 6
AHEAD = 2
LATE = [(2, "out", 6), (2, "in", 4), (4, "out", 7), (4, "in", 5), (6, "in", 6), (8, "in", 7)]

OUT, IN_SIDE, IN_NEAR, IN_FAR, USE, MIRROR, LIVE, LEFT, PAIRS, ROWS = 0, 1, 2, 3, 4, 6, 8, 10, 12, 16


def bit_count(value):
    value = value - ((value >> 1) & 0x5555)
    value = (value & 0x3333) + ((value >> 2) & 0x3333)
    value = (value + (value >> 4)) & 0x0F0F
    return (value + (value >> 8)) & 0x1F


def power(place):
    return jnp.left_shift(1, place)


def bit_rank(mask, place):
    return bit_count(mask & (power(place) - 1))


def set_bits(mask, count, spare):
    places = []
    for _ in range(count):
        low = mask & -mask
        places.append(jnp.where(mask == 0, spare, bit_count(low - 1)))
        mask = mask & (mask - 1)
    return places


def row_masks(screen, lengths, count_va, slots):
    def one(m, masks):
        return tuple(
            mask | jnp.where(m < lengths[row], power(jnp.maximum(screen[row, m], 0)), 0) for row, mask in enumerate(masks)
        )

    return lax.fori_loop(0, slots, one, (jnp.int32(0),) * count_va)


def level_tiles(level, per_level):
    return ((1 << per_level) - 1) << (level * per_level)


def any_of(masks):
    return functools.reduce(lambda one, two: one | two, masks)


def link_masks(masks, levels, per_level):
    wanted = [any_of(masks[level * PAIR : (level + 1) * PAIR]) for level in range(levels)]
    half = levels // 2
    end_out, mid_out, end_in = [], [], []
    for side in range(2):
        end = 0 if side == 0 else levels - 1
        mine = range(half) if side == 0 else range(half, levels)
        end_tiles = level_tiles(end, per_level)
        end_out.append(end_tiles & any_of([wanted[l] for l in range(levels) if l != end]))
        mid_out.append(
            any_of([level_tiles(l, per_level) for l in mine]) & any_of([wanted[l] for l in range(levels) if l not in mine])
        )
        end_in.append(wanted[end] & ~end_tiles)
    return end_out, mid_out, end_in


def pair_mask(low, high, level, per_level):
    every = (1 << per_level) - 1
    return ((low >> (level * per_level)) & every) | (((high >> (level * per_level)) & every) << per_level)


def listed_kernel(caps, slots, table_ref, occ_ref, amp_ref, int_ref, rows_from, cols_from, out_ref, *refs):
    first_cap, mid_cap, end_cap, pair_cap = caps
    refs = list(refs)
    count_va = lax.axis_size("va")
    levels = count_va // PAIR
    occ_count = amp_ref.shape[0]
    own_tiles = int_ref.shape[1]
    rows = own_tiles * TILE
    cols = int_ref.shape[3]
    per_level = own_tiles * PAIR
    col_parts = cols // TILE
    units = occ_count * col_parts
    pairs = slots + slots // 2
    group = pairs // GROUPS

    near = [refs.pop(0) for _ in range(units)]
    far = [refs.pop(0) for _ in range(units)]
    out_pack = [refs.pop(0) for _ in range(units)]
    in_pack = [refs.pop(0) for _ in range(units)]
    share, sib, mirror_out, mirror_in, spin_mine, spin_other = [
        [refs.pop(0) for _ in range(PAIR)] for _ in range(6)
    ]
    (
        lefts, rights, vir_rows, part_own, part_out, part_in, table, occ, rows_ref, cols_ref, load_sem, near_sem, own_sem,
        y_send, y_recv, out_send, near_recv, far_recv, in_send, a_send, a_recv, sib_send, sib_recv, m_send, m_recv,
        x_send, x_recv, c_send, c_recv, p_send, p_recv,
    ) = refs

    va = lax.axis_index("va")
    vb = lax.axis_index("vb")
    z, y = va // PAIR, va % PAIR
    x, c = vb // PAIR, vb % PAIR
    upper = z // (levels // 2)
    inner = jnp.where(upper == 0, z, levels - 1 - z)
    toward = jnp.where(upper == 0, PAIR, -PAIR)
    end_level = jnp.where(upper == 0, 0, levels - 1)
    lead = z % PAIR
    own_at = per_level + y * own_tiles

    def remote(src, dst, send, recv, target):
        return pltpu.make_async_remote_copy(
            src_ref=src, dst_ref=dst, send_sem=send, recv_sem=recv, device_id=target, device_id_type=MESH
        )

    def tile_rows(begin):
        return pl.ds(pl.multiple_of(begin * TILE, TILE), TILE)

    def unit(u):
        return u // col_parts, pl.ds(u % col_parts * TILE, TILE)

    def y_copy(u):
        j, at = unit(u)
        return remote(
            int_ref.at[(1 - y) * occ_count + j, :, :, at], near[u].at[pl.ds(own_at, own_tiles)],
            y_send.at[u], y_recv.at[u], {"va": z * PAIR + 1 - y},
        )

    def y_arrival(u):
        here = near[u].at[pl.ds(per_level + (1 - y) * own_tiles, own_tiles)]
        return remote(here, here, y_send.at[u], y_recv.at[u], {"va": va})

    flips = [(1, 0), (0, 1), (1, 1)]

    def flipped(f):
        flip_x, flip_y = flips[f]
        return x + flip_x * (1 - 2 * x), y + flip_y * (1 - 2 * y)

    def block_tiles(at_x, at_y, side):
        return pl.ds(((at_x * PAIR + at_y) * PAIR + side) * own_tiles, own_tiles)

    def half_cols(side, half):
        return pl.ds((side * PAIR + half) * TILE, TILE)

    def share_copy(half, f, side):
        to_x, to_y = flipped(f)
        return remote(
            amp_ref.at[to_x, to_y, :, :, half_cols(side, half)], share[half].at[block_tiles(x, y, side)],
            a_send.at[half, f, side], a_recv.at[half, f, side], {"va": z * PAIR + to_y, "vb": to_x * PAIR + c},
        )

    def share_arrival(half, f, side):
        here = share[half].at[block_tiles(*flipped(f), side)]
        return remote(here, here, a_send.at[half, f, side], a_recv.at[half, f, side], {"va": va})

    def each_share(act):
        for f in range(3):
            for side in range(PAIR):
                act(f, side)

    loads = [
        pltpu.make_async_copy(src, dst, load_sem.at[n])
        for n, (src, dst) in enumerate(
            [
                (table_ref, table), (occ_ref, occ),
                (rows_from.at[va], rows_ref), (cols_from.at[vb], cols_ref),
            ]
        )
    ]

    def near_own(u):
        j, at = unit(u)
        return pltpu.make_async_copy(
            int_ref.at[y * occ_count + j, :, :, at], near[u].at[pl.ds(own_at, own_tiles)], near_sem.at[u]
        )

    def share_own(half, side):
        return pltpu.make_async_copy(
            amp_ref.at[x, y, :, :, half_cols(side, half)], share[half].at[block_tiles(x, y, side)], own_sem.at[half, side]
        )

    for load in loads:
        load.start()
    for u in range(units):
        near_own(u).start()
    for half in range(PAIR):
        for side in range(PAIR):
            share_own(half, side).start()

    barrier = pltpu.get_barrier_semaphore()
    partners = [{"vb": x * PAIR + 1 - c}]
    for f in range(3):
        to_x, to_y = flipped(f)
        partners.append({"va": z * PAIR + to_y, "vb": to_x * PAIR + c})
    for step in range(1, levels):
        partners.append({"va": lax.rem(z + step, levels) * PAIR + y})
    for partner in partners:
        pl.semaphore_signal(barrier, inc=1, device_id=partner, device_id_type=MESH)
    pl.semaphore_wait(barrier, len(partners))

    y_copy(0).start()

    for load in loads:
        load.wait()
    vir_rows[...] = jnp.broadcast_to(rows_ref[...], (TILE, rows)).T

    def out_copy(u, end):
        if end:
            here, there = out_pack[u].at[pl.ds(0, first_cap)], near[u].at[pl.ds(0, first_cap)]
            return remote(here, there, out_send.at[u], near_recv.at[u], {"va": va + toward})
        here, there = out_pack[u].at[pl.ds(0, mid_cap)], far[u].at[pl.ds(0, mid_cap)]
        return remote(here, there, out_send.at[u], far_recv.at[u], {"va": va + toward})

    def near_arrival(u):
        here = near[u].at[pl.ds(0, first_cap)]
        return remote(here, here, out_send.at[u], near_recv.at[u], {"va": va})

    def far_arrival(u, end):
        here = far[u].at[pl.ds(0, end_cap if end else mid_cap)]
        return remote(here, here, out_send.at[u], far_recv.at[u], {"va": va})

    def in_copy(u):
        here, there = in_pack[u].at[pl.ds(0, end_cap)], far[u].at[pl.ds(0, end_cap)]
        return remote(here, there, in_send.at[u], far_recv.at[u], {"va": va - toward})

    def y_wait(u):
        y_arrival(u).wait_recv()

    def share_start(half):
        each_share(lambda f, side: share_copy(half, f, side).start())

    def out_step(u):
        near_own(u).wait()
        if u:
            y_wait(u)

        @pl.when(inner == 1)
        def _():
            near_arrival(u).wait_recv()

        @functools.partial(lax.fori_loop, 0, max(first_cap, mid_cap), init_val=0)
        def _(s, carry):
            out_pack[u][s] = near[u][table[OUT, s]]
            return carry

        for end in (True, False):

            @pl.when(inner == (0 if end else 1))
            def _():
                if u >= AHEAD:
                    out_copy(u - AHEAD, end).wait_send()
                out_copy(u, end).start()

    def in_step(u):
        @pl.when(inner == 1)
        def _():
            far_arrival(u, False).wait_recv()

            @functools.partial(lax.fori_loop, 0, end_cap, init_val=0)
            def _(s, carry):
                in_pack[u][s] = jnp.where(
                    table[IN_SIDE, s] == 1, near[u][table[IN_NEAR, s]], far[u][table[IN_FAR, s]]
                )
                return carry

            in_copy(u).start()

    def sib_copy(half):
        return remote(share[half], sib[half], sib_send.at[half], sib_recv.at[half], {"vb": x * PAIR + 1 - c})

    def sib_arrival(half):
        return remote(sib[half], sib[half], sib_send.at[half], sib_recv.at[half], {"vb": vb})

    def mirror_copy(half, at_x):
        level = at_x * PAIR + c
        return remote(
            mirror_out[half].at[pl.ds(at_x * pair_cap, pair_cap)],
            mirror_in[half].at[pl.ds(z * pair_cap, pair_cap)],
            m_send.at[half, at_x], m_recv.at[half, z], {"va": level * PAIR + y},
        )

    def mirror_arrival(half, level):
        here = mirror_in[half].at[pl.ds(level * pair_cap, pair_cap)]
        return remote(here, here, m_send.at[half, 0], m_recv.at[half, level], {"va": va})

    def share_step(half):
        each_share(lambda f, side: share_arrival(half, f, side).wait_recv())
        for side in range(PAIR):
            share_own(half, side).wait()
        for at_x in range(PAIR):
            level = at_x * PAIR + c

            @functools.partial(lax.fori_loop, 0, pair_cap, init_val=0)
            def _(s, carry):
                place = table[MIRROR + at_x, s]
                side, tile = place // per_level, place % per_level
                block = (at_x * PAIR + tile // own_tiles) * PAIR + side
                mirror_out[half][at_x * pair_cap + s] = share[half][block * own_tiles + tile % own_tiles]
                return carry

            @pl.when(level != z)
            def _():
                mirror_copy(half, at_x).start()

            @pl.when(level == z)
            def _():
                mirror_in[half][pl.ds(z * pair_cap, pair_cap)] = mirror_out[half][
                    pl.ds(at_x * pair_cap, pair_cap)
                ]

        @pl.when(c != lead)
        def _():
            sib_copy(half).start()

    def spin_group(ref, g):
        return ref.at[pl.ds(g * group, group)]

    def x_copy(half, g):
        return remote(
            spin_group(spin_mine[half], g), spin_group(spin_other[half], g), x_send.at[half, g], x_recv.at[half, g],
            {"vb": (1 - x) * PAIR + c},
        )

    def x_arrival(half, g):
        here = spin_group(spin_other[half], g)
        return remote(here, here, x_send.at[half, g], x_recv.at[half, g], {"vb": vb})

    def core_copy(which, half, g):
        ref = (spin_mine, spin_other)[which][half]
        return remote(
            spin_group(ref, g), spin_group(ref, g), c_send.at[which, half, g], c_recv.at[which, half, g],
            {"vb": x * PAIR + 1 - c},
        )

    def core_arrival(which, half, g):
        here = spin_group((spin_mine, spin_other)[which][half], g)
        return remote(here, here, c_send.at[which, half, g], c_recv.at[which, half, g], {"vb": vb})

    def spin_step(half):
        @pl.when(c == lead)
        def _():
            for level in range(levels):

                @pl.when(level != z)
                def _():
                    mirror_arrival(half, level).wait_recv()

            if half == 0:
                for one in range(PAIR):
                    sib_arrival(one).wait_recv()
            for g in range(GROUPS):

                @functools.partial(lax.fori_loop, g * group, (g + 1) * group, init_val=0)
                def _(q, carry):
                    side, tile, place = table[PAIRS, q], table[PAIRS + 1, q], table[PAIRS + 2, q] * pair_cap + table[PAIRS + 3, q]
                    owner, within = tile // col_parts, tile % col_parts
                    block = ((owner // PAIR) * PAIR + side) * PAIR + within // PAIR
                    at = block * own_tiles + half
                    first, second = [
                        jnp.where(owner % PAIR == lead, share[one][at], sib[one][at]) for one in range(PAIR)
                    ]
                    own = jnp.where(within % PAIR == 0, first, second)
                    mirror = mirror_in[half][place]
                    spin = 2.0 * own.astype(jnp.float32) - mirror.astype(jnp.float32).T
                    spin_mine[half][q] = spin.astype(amp_ref.dtype)
                    return carry

                x_copy(half, g).start()
                core_copy(0, half, g).start()

    def pass_step(half):
        @pl.when(c == lead)
        def _():
            for g in range(GROUPS):
                x_arrival(half, g).wait_recv()
                core_copy(1, half, g).start()

    def left_step(half):
        @pl.when(c != lead)
        def _():
            for g in range(GROUPS):
                for which in range(2):
                    core_arrival(which, half, g).wait_recv()

        @functools.partial(lax.fori_loop, 0, PAIR * slots, init_val=0)
        def _(index, carry):
            side, m = index // slots, index % slots
            live = table[LIVE + side, m] == 1
            q = table[LEFT + side, m]
            lanes = pl.ds(pl.multiple_of(m * TILE, TILE), TILE)
            for ref, place in ((spin_mine, x), (spin_other, 1 - x)):
                value = ref[half][q]
                lefts[half, side, tile_rows(place), lanes] = jnp.where(live, value, jnp.zeros_like(value))
            return carry

    def part_copy(u, half):
        return remote(
            part_out.at[u, half], part_in.at[u, half], p_send.at[u, half], p_recv.at[u, half], {"va": z * PAIR + 1 - y}
        )

    def part_arrival(u, half):
        return remote(part_in.at[u, half], part_in.at[u, half], p_send.at[u, half], p_recv.at[u, half], {"va": va})

    def end_wait(u):
        @pl.when(inner == 0)
        def _():
            far_arrival(u, True).wait_recv()

    def gather_step(u):
        @functools.partial(lax.fori_loop, 0, PAIR * slots, init_val=0)
        def _(index, carry):
            side, m = index // slots, index % slots
            place = table[USE + side, m]
            here = jnp.minimum(place, 2 * per_level - 1)
            there = jnp.maximum(place - 2 * per_level, 0)
            rights[u, side, tile_rows(m), :] = jnp.where(place < 2 * per_level, near[u][here], far[u][there])
            return carry

    def dot_step(u, half):
        total = jnp.dot(lefts[half, 1 - y], rights[u, 1 - y], preferred_element_type=jnp.float32)
        part_out[u, half] = total.astype(part_out.dtype)
        part_copy(u, half).start()
        part_own[u, half] = jnp.dot(lefts[half, y], rights[u, y], preferred_element_type=jnp.float32)

    def final_step(u, half):
        j = u // col_parts
        at = pl.ds(pl.multiple_of(u % col_parts * TILE, TILE), TILE)
        part_arrival(u, half).wait_recv()
        part_rows = tile_rows(half)
        for i in range(occ_count):
            bottom = (occ[i] + occ[j] - vir_rows[part_rows, :]) - cols_ref[:, at]
            here = pl.ds(i * TILE, TILE)
            whole = part_own[u, half, here, :] + part_in[u, half, here, :].astype(jnp.float32)
            out_ref[i, j, part_rows, at] = whole / bottom

    def y_start(u):
        if u < units:
            y_copy(u).start()

    y_wait(0)
    share_start(0)
    y_start(1)
    out_step(0)
    share_step(0)
    share_start(1)
    y_start(2)
    out_step(1)
    y_start(3)
    share_step(1)
    y_start(4)
    out_step(2)
    in_step(0)
    y_start(5)
    out_step(3)
    in_step(1)
    y_start(6)
    spin_step(0)
    y_start(7)
    out_step(4)
    in_step(2)
    pass_step(0)
    spin_step(1)
    out_step(5)
    in_step(3)
    left_step(0)

    stages = units * PAIR
    early = units // 2

    def place_of(stage):
        first = stage < early * PAIR
        u = jnp.where(first, stage % early, stage // PAIR)
        return u, jnp.where(first, stage // early, stage % PAIR)

    actions = {stage: [] for stage in range(stages)}
    for u in range(units):
        stage = u if u < early else early * PAIR + (u - early) * PAIR
        actions[stage] += [functools.partial(end_wait, u), functools.partial(gather_step, u)]
    actions[early] = [functools.partial(pass_step, 1), functools.partial(left_step, 1), *actions[early]]
    for stage, step, u in LATE:
        actions[stage] = [functools.partial({"in": in_step, "out": out_step}[step], u), *actions[stage]]

    @functools.partial(lax.fori_loop, 0, stages, init_val=0)
    def _(stage, carry):
        for at, acts in actions.items():
            if acts:

                @pl.when(stage == at)
                def _():
                    for act in acts:
                        act()

        dot_step(*place_of(stage))

        @pl.when(stage >= LAG)
        def _():
            final_step(*place_of(stage - LAG))

        return carry

    @functools.partial(lax.fori_loop, stages - LAG, stages, init_val=0)
    def _(stage, carry):
        final_step(*place_of(stage))
        return carry

    for u in range(units):
        y_copy(u).wait_send()
        for half in range(PAIR):
            part_copy(u, half).wait_send()

        @pl.when(inner == 1)
        def _():
            in_copy(u).wait_send()

        if u >= units - AHEAD:
            for end in (True, False):

                @pl.when(inner == (0 if end else 1))
                def _():
                    out_copy(u, end).wait_send()

    for half in range(PAIR):
        each_share(lambda f, side: share_copy(half, f, side).wait_send())
        for at_x in range(PAIR):

            @pl.when(at_x * PAIR + c != z)
            def _():
                mirror_copy(half, at_x).wait_send()

        @pl.when(c != lead)
        def _():
            sib_copy(half).wait_send()

        @pl.when(c == lead)
        def _():
            for g in range(GROUPS):
                x_copy(half, g).wait_send()
                for which in range(2):
                    core_copy(which, half, g).wait_send()


def listed_all(index, caps, slots, amplitudes, integrals, occ_energy, vir_energy, table):
    first_cap, mid_cap, end_cap, pair_cap = caps
    count_va = lax.axis_size("va")
    count_vb = lax.axis_size("vb")
    occ_a, occ_b, row_len, col_len = amplitudes.shape
    blocks, rows, cols = integrals.shape
    levels = count_va // PAIR
    own_tiles = rows // TILE
    per_level = own_tiles * PAIR
    units = occ_a * (cols // TILE)
    pairs = slots + slots // 2
    kind = amplitudes.dtype
    dma = pltpu.SemaphoreType.DMA
    vmem = pltpu.VMEM
    return pl.pallas_call(
        functools.partial(listed_kernel, caps, slots),
        out_shape=jax.ShapeDtypeStruct((occ_a, occ_b, row_len, cols), jnp.float32),
        in_specs=[pl.BlockSpec(memory_space=pl.ANY)] * 6,
        out_specs=pl.BlockSpec(memory_space=vmem),
        scratch_shapes=[
            *[vmem((2 * per_level, TILE, TILE), kind)] * units,
            *[vmem((max(mid_cap, end_cap), TILE, TILE), kind)] * units,
            *[vmem((max(first_cap, mid_cap), TILE, TILE), kind)] * units,
            *[vmem((end_cap, TILE, TILE), kind)] * units,
            *[vmem((PAIR * PAIR * PAIR * own_tiles, TILE, TILE), kind)] * (2 * PAIR),
            *[vmem((PAIR * pair_cap, TILE, TILE), kind)] * PAIR,
            *[vmem((levels * pair_cap, TILE, TILE), kind)] * PAIR,
            *[vmem((pairs, TILE, TILE), kind)] * (2 * PAIR),
            vmem((PAIR, PAIR, occ_a * TILE, slots * TILE), kind),
            vmem((units, PAIR, slots * TILE, TILE), kind),
            vmem((rows, TILE), jnp.float32),
            vmem((units, PAIR, occ_a * TILE, TILE), jnp.float32),
            vmem((units, PAIR, occ_a * TILE, TILE), kind),
            vmem((units, PAIR, occ_a * TILE, TILE), kind),
            pltpu.SMEM(table.shape, table.dtype),
            pltpu.SMEM(occ_energy.shape, occ_energy.dtype),
            vmem((1, row_len), jnp.float32),
            vmem((1, cols), jnp.float32),
            dma((4,)),
            dma((units,)),
            dma((PAIR, PAIR)),
            *[dma((units,))] * 6,
            *[dma((PAIR, 3, PAIR))] * 2,
            *[dma((PAIR,))] * 2,
            dma((PAIR, PAIR)), dma((PAIR, levels)),
            *[dma((PAIR, GROUPS))] * 2,
            *[dma((2, PAIR, GROUPS))] * 2,
            *[dma((units, PAIR))] * 2,
        ],
        compiler_params=pltpu.CompilerParams(collective_id=index, has_side_effects=True, vmem_limit_bytes=60 * 2**20),
    )(
        table, occ_energy, amplitudes.reshape(occ_a, occ_b, own_tiles, TILE, col_len),
        integrals.reshape(blocks, own_tiles, TILE, cols),
        vir_energy.reshape(count_va, 1, row_len), vir_energy.reshape(count_vb, 1, cols),
    )


def fits(amplitudes, integrals, screen, count_va, count_vb):
    levels = count_va // PAIR
    rows, cols = integrals.shape[1:]
    return (
        levels == PAIR * PAIR
        and count_vb == levels
        and amplitudes.shape[0] == PAIR
        and rows == PAIR * TILE
        and cols == PAIR * rows
        and count_va * rows == ROWS * TILE
        and screen.shape[1] % 4 == 0
    )


def dense(amplitudes, integrals, occ_energy, vir_energy, screen, lengths):
    count_va = lax.axis_size("va")
    count_vb = lax.axis_size("vb")
    occ_a, occ_b, row_len, col_len = amplitudes.shape
    cols = integrals.shape[2]
    whole_k, spin_all = gather_all(amplitudes, integrals, count_va, count_vb)
    slots = screen.shape[1]
    per_shard = col_len // TILE
    at = jnp.stack([lax.axis_index("va"), lax.axis_index("vb")]).astype(jnp.int32)

    def tile_of(m, at, screen, lengths):
        return jnp.maximum(screen[at[0], jnp.minimum(m, lengths[at[0]] - 1)], 0)

    def spin_at(place, m, at, screen, lengths, occ):
        tile = tile_of(m * GROUP + place, at, screen, lengths)
        return (tile // per_shard, 0, 0, 0, tile % per_shard)

    def k_at(place, m, at, screen, lengths, occ):
        return (0, tile_of(m * GROUP + place, at, screen, lengths), 0)

    return pl.pallas_call(
        cycle_kernel,
        out_shape=jax.ShapeDtypeStruct((occ_a, occ_b, row_len, cols), jnp.float32),
        grid_spec=pltpu.PrefetchScalarGridSpec(
            num_scalar_prefetch=4,
            grid=(pl.cdiv(slots, GROUP),),
            in_specs=[
                *(
                    pl.BlockSpec((1, occ_a, occ_b, row_len, TILE), functools.partial(spin_at, place))
                    for place in range(GROUP)
                ),
                *(
                    pl.BlockSpec((integrals.shape[0], TILE, cols), functools.partial(k_at, place))
                    for place in range(GROUP)
                ),
                pl.BlockSpec((1, 1, row_len), lambda m, at, screen, lengths, occ: (at[0], 0, 0)),
                pl.BlockSpec((1, 1, cols), lambda m, at, screen, lengths, occ: (at[1], 0, 0)),
            ],
            out_specs=pl.BlockSpec(
                (occ_a, occ_b, row_len, cols), lambda m, at, screen, lengths, occ: (0, 0, 0, 0)
            ),
        ),
    )(
        at, screen, lengths, occ_energy, *[spin_all] * GROUP, *[whole_k] * GROUP,
        vir_energy.reshape(count_va, 1, row_len), vir_energy.reshape(count_vb, 1, cols),
    )


CAPS = ((4, 5, 5, 5), (4, 6, 6, 5), (4, 7, 7, 5), (4, 8, 8, 6), (4, 8, 9, 6), (4, 8, 12, 8))


def plan_kernel(caps, per_level, screen_ref, lengths_ref, choice, table, screen, lengths, load_sem):
    loads = [
        pltpu.make_async_copy(src, dst, load_sem.at[n])
        for n, (src, dst) in enumerate([(screen_ref, screen), (lengths_ref, lengths)])
    ]
    for load in loads:
        load.start()
    for load in loads:
        load.wait()
    count_va, slots = screen.shape
    levels = count_va // PAIR
    tiles = levels * per_level
    pairs = slots + slots // 2
    z = lax.axis_index("va") // PAIR
    c = lax.axis_index("vb") % PAIR
    upper = z // (levels // 2)
    inner = jnp.where(upper == 0, z, levels - 1 - z)
    end_level = jnp.where(upper == 0, 0, levels - 1)

    masks = row_masks(screen, lengths, count_va, slots)
    end_out, mid_out, end_in = [
        (jnp.where(upper == 0, one[0], one[1]), jnp.where(upper == 0, one[1], one[0]))
        for one in link_masks(masks, levels, per_level)
    ]

    arrives = jnp.where(inner == 1, mid_out[1], end_in[0])

    def place_of(tile):
        level = tile // per_level
        own = level == z
        from_end = jnp.logical_and(inner == 1, level == end_level)
        rank = bit_rank(jnp.where(from_end, end_out[0], arrives), tile)
        is_near = jnp.logical_or(own, from_end)
        return is_near, jnp.where(own, per_level + tile % per_level, rank)

    spare = z * per_level
    for s, tile in enumerate(set_bits(jnp.where(inner == 1, mid_out[0], end_out[0]), per_level * PAIR, spare)):
        table[OUT, s] = place_of(tile)[1]
    for s, tile in enumerate(set_bits(end_in[0], tiles - per_level, spare)):
        is_near, place = place_of(tile)
        table[IN_SIDE, s] = is_near.astype(jnp.int32)
        table[IN_NEAR, s] = jnp.where(is_near, place, per_level)
        table[IN_FAR, s] = jnp.where(is_near, 0, place)

    def of_level(level, side):
        mask = masks[side]
        for l in range(1, levels):
            mask = jnp.where(level == l, masks[l * PAIR + side], mask)
        return mask

    for at_x in range(PAIR):
        level = at_x * PAIR + c
        mask = pair_mask(of_level(level, 0), of_level(level, 1), z, per_level)
        for s, place in enumerate(set_bits(mask, per_level * PAIR, 0)):
            table[MIRROR + at_x, s] = place

    own_masks = [of_level(z, side) for side in range(PAIR)]
    counts = [lengths[z * PAIR + side] for side in range(PAIR)]

    def own_count(side):
        return jnp.where(side == 0, counts[0], counts[1])

    @functools.partial(lax.fori_loop, 0, pairs, init_val=0)
    def _(q, carry):
        side = (q >= counts[0]).astype(jnp.int32)
        m = jnp.clip(jnp.where(side == 0, q, q - counts[0]), 0, slots - 1)
        tile = jnp.maximum(screen[z * PAIR + side, m], 0)
        level = tile // per_level
        mask = pair_mask(own_masks[0], own_masks[1], level, per_level)
        rank = bit_rank(mask, side * per_level + tile % per_level)
        table[PAIRS, q] = side
        table[PAIRS + 1, q] = tile
        table[PAIRS + 2, q] = level
        table[PAIRS + 3, q] = rank
        return carry

    @functools.partial(lax.fori_loop, 0, PAIR * slots, init_val=0)
    def _(index, carry):
        side, m = index // slots, index % slots
        tile = jnp.maximum(screen[z * PAIR + side, jnp.clip(own_count(side) - 1, 0, m)], 0)
        is_near, place = place_of(tile)
        table[USE + side, m] = jnp.where(is_near, place, 2 * per_level + place)
        table[LIVE + side, m] = (m < own_count(side)).astype(jnp.int32)
        table[LEFT + side, m] = jnp.minimum(jnp.where(side == 0, m, counts[0] + m), pairs - 1)
        return carry

    middle = jnp.maximum(*map(bit_count, mid_out))
    ends = jnp.maximum(*map(bit_count, end_in))
    most = functools.reduce(
        jnp.maximum,
        [
            bit_count(pair_mask(masks[PAIR * to], masks[PAIR * to + 1], level, per_level))
            for to in range(levels)
            for level in range(levels)
        ],
    )
    chosen = jnp.int32(len(caps) - 1)
    for index, (_, mid_cap, end_cap, pair_cap) in reversed(list(enumerate(caps[:-1]))):
        enough = jnp.logical_and(jnp.logical_and(middle <= mid_cap, ends <= end_cap), most <= pair_cap)
        chosen = jnp.where(enough, index, chosen)
    choice[0] = chosen


def plan(screen, lengths, per_level):
    return pl.pallas_call(
        functools.partial(plan_kernel, CAPS, per_level),
        out_shape=(jax.ShapeDtypeStruct((1,), jnp.int32), jax.ShapeDtypeStruct((ROWS, ROWS), jnp.int32)),
        in_specs=[pl.BlockSpec(memory_space=pl.ANY)] * 2,
        out_specs=(pl.BlockSpec(memory_space=pltpu.SMEM),) * 2,
        scratch_shapes=[
            pltpu.SMEM(screen.shape, screen.dtype),
            pltpu.SMEM(lengths.shape, lengths.dtype),
            pltpu.SemaphoreType.DMA((2,)),
        ],
        compiler_params=pltpu.CompilerParams(vmem_limit_bytes=60 * 2**20),
    )(screen, lengths)


def local(amplitudes, integrals, occ_energy, vir_energy, screen, lengths):
    operands = (amplitudes, integrals, occ_energy, vir_energy, screen, lengths)
    if not fits(amplitudes, integrals, screen, lax.axis_size("va"), lax.axis_size("vb")):
        return dense(*operands)
    choice, table = plan(screen, lengths, integrals.shape[1] // TILE * PAIR)
    branches = [functools.partial(listed_all, index, caps, screen.shape[1]) for index, caps in enumerate(CAPS)]
    return lax.switch(choice[0], branches, amplitudes, integrals, occ_energy, vir_energy, table)


def solution(mesh):
    return jax.shard_map(
        local,
        mesh=mesh,
        in_specs=(P(None, None, "va", "vb"), P(None, "va", "vb"), P(), P(), P(), P()),
        out_specs=P(None, None, "va", "vb"),
        check_vma=False,
    )
```

```python
import functools

import jax
import jax.numpy as jnp
from jax import lax
from jax.experimental import pallas as pl
from jax.experimental.pallas import tpu as pltpu
from jax.sharding import PartitionSpec as P

TILE = 128
PAIR = 2
SPLIT = 2
GROUP = 2
MESH = pl.DeviceIdType.MESH


def gather_kernel(
    count_va, count_vb, flip, amp_ref, *refs
):
    refs = list(refs)
    turned_ref = None if flip else refs.pop(0)
    (
        int_ref, whole_k, spin_all,
        landed, passing, spin, z_send, z_recv, y_send, y_recv, m_send, m_recv, x_send, x_recv, s_send, s_recv, own_sem,
    ) = refs
    va = lax.axis_index("va")
    vb = lax.axis_index("vb")
    ratio = count_va // count_vb
    lines = count_va // PAIR
    outers = count_vb // PAIR
    line, side = va // PAIR, va % PAIR
    outer, core = vb // PAIR, vb % PAIR
    blocks, rows, _ = int_ref.shape
    part_rows = rows // SPLIT
    chunks = blocks * SPLIT
    early = chunks - 1
    halves = amp_ref.shape[0]
    row_len = amp_ref.shape[2]

    def k_slot(owner, chunk):
        begin = owner * rows + chunk % SPLIT * part_rows
        return whole_k.at[chunk // SPLIT, pl.ds(pl.multiple_of(begin, part_rows), part_rows)]

    def own_slot(chunk):
        return int_ref.at[chunk // SPLIT, pl.ds(chunk % SPLIT * part_rows, part_rows)]

    def remote(src, dst, send, recv, target):
        return pltpu.make_async_remote_copy(
            src_ref=src, dst_ref=dst, send_sem=send, recv_sem=recv, device_id=target, device_id_type=MESH
        )

    next_vb = lax.rem(outer + 1, outers) * PAIR + core
    last_vb = lax.rem(outer + outers - 1, outers) * PAIR + core

    def by_relay(half):
        return outers > 1 and half % 2 == 1

    def piece(part):
        if flip:
            return amp_ref.at[:, :, :, pl.ds(part * row_len, row_len)]
        return turned_ref.at[part]

    def half_piece(part, half):
        if flip:
            return amp_ref.at[half, :, :, pl.ds(part * row_len, row_len)]
        return turned_ref.at[part, half]

    def mirror_own(part):
        return pltpu.make_async_copy(piece(part), landed.at[part], own_sem.at[part])

    def mirror_straight(part, half):
        return remote(
            half_piece(part, half), landed.at[va % ratio, half],
            m_send.at[0, part, half], m_recv.at[va % ratio, half],
            {"va": vb * ratio + part, "vb": va // ratio},
        )

    def mirror_out(part, half):
        return remote(
            half_piece(part, half), passing.at[part, half],
            x_send.at[part, half], x_recv.at[part, half], {"vb": next_vb},
        )

    def mirror_on(part, half):
        return remote(
            passing.at[part, half], landed.at[va % ratio, half],
            m_send.at[1, part, half], m_recv.at[va % ratio, half],
            {"va": last_vb * ratio + part, "vb": va // ratio},
        )

    def mirror_passing(part, half):
        here = passing.at[part, half]
        return remote(here, here, x_send.at[part, half], x_recv.at[part, half], {"vb": vb})

    def mirror_arrival(part, half):
        here = landed.at[part, half]
        return remote(here, here, m_send.at[0, part, half], m_recv.at[part, half], {"vb": vb})

    def stays(part):
        return va == vb * ratio + part

    def last_stays(part):
        return va == last_vb * ratio + part

    def each_mirror(own, straight, out):
        for part in range(ratio):

            @pl.when(stays(part))
            def _():
                own(part)

            @pl.when(jnp.logical_not(stays(part)))
            def _():
                for half in range(halves):
                    (out if by_relay(half) else straight)(part, half)

    each_mirror(
        lambda part: mirror_own(part).start(),
        lambda part, half: mirror_straight(part, half).start(),
        lambda part, half: mirror_out(part, half).start(),
    )

    def each_passing(act):
        for part in range(ratio):

            @pl.when(jnp.logical_not(last_stays(part)))
            def _():
                for half in range(halves):
                    if by_relay(half):
                        act(part, half)

    def source(direction, step):
        return line - step if direction == 0 else line + step

    def line_slot(direction, step, chunk):
        if chunk == chunks:
            return k_slot(source(direction, step) * PAIR + 1 - side, early)
        return k_slot(source(direction, step) * PAIR + side, chunk)

    def block_at(direction, step, chunk):
        if step == 0 and chunk < chunks:
            return own_slot(chunk)
        return line_slot(direction, step, chunk)

    def line_send(direction, step, chunk):
        to = line + 1 if direction == 0 else line - 1
        return remote(
            block_at(direction, step, chunk),
            line_slot(direction, step, chunk),
            z_send.at[direction, step, chunk],
            z_recv.at[direction, step, chunk],
            {"va": to * PAIR + side},
        )

    def line_arrival(direction, step, chunk):
        here = line_slot(direction, step, chunk)
        return remote(
            here, here, z_send.at[direction, step - 1, chunk], z_recv.at[direction, step - 1, chunk],
            {"va": va},
        )

    def may_send(direction, step):
        if direction == 0:
            return jnp.logical_and(line - step >= 0, line + 1 < lines)
        return jnp.logical_and(line + step < lines, line - 1 >= 0)

    def has_arrival(direction, step):
        return line - step >= 0 if direction == 0 else line + step < lines

    def side_send(direction, step, chunk):
        return remote(
            block_at(direction, step, chunk),
            line_slot(direction, step, chunk),
            y_send.at[direction, step, chunk],
            y_recv.at[direction, step, chunk],
            {"va": line * PAIR + 1 - side},
        )

    def side_arrival(direction, step, chunk):
        here = k_slot(source(direction, step) * PAIR + 1 - side, chunk)
        return remote(
            here, here, y_send.at[direction, step, chunk], y_recv.at[direction, step, chunk], {"va": va}
        )

    def own_copy(chunk):
        return pltpu.make_async_copy(own_slot(chunk), k_slot(va, chunk), own_sem.at[ratio + 1 + chunk])

    def send_own(chunk):
        for direction in range(2):

            @pl.when(may_send(direction, 0))
            def _():
                line_send(direction, 0, chunk).start()

    side_send(0, 0, early).start()
    for chunk in range(chunks):
        send_own(chunk)
        if chunk != early:
            side_send(0, 0, chunk).start()
    for chunk in range(chunks):
        own_copy(chunk).start()
    side_arrival(0, 0, early).wait_recv()
    send_own(chunks)

    def pass_mirror(part, half):
        mirror_passing(part, half).wait_recv()
        mirror_on(part, half).start()

    each_passing(pass_mirror)

    def line_step(step):
        for chunk in range(chunks + 1):
            for direction in range(2):

                @pl.when(has_arrival(direction, step))
                def _():
                    line_arrival(direction, step, chunk).wait_recv()

                    @pl.when(may_send(direction, step))
                    def _():
                        line_send(direction, step, chunk).start()

                    if chunk < early:
                        side_send(direction, step, chunk).start()

    def spin_send(shift):
        to = lax.rem(outer + shift, outers)
        return remote(
            spin, spin_all.at[vb], s_send.at[0, shift], s_recv.at[0, shift], {"vb": to * PAIR + core}
        )

    def spin_arrival(shift):
        here = spin_all.at[lax.rem(outer + outers - shift, outers) * PAIR + core]
        return remote(here, here, s_send.at[0, shift], s_recv.at[0, shift], {"vb": vb})

    def spin_relay(shift):
        held = spin_all.at[lax.rem(outer + outers - shift, outers) * PAIR + core]
        src = spin if shift == 0 else held
        return remote(
            src, held, s_send.at[1, shift], s_recv.at[1, shift], {"vb": outer * PAIR + 1 - core}
        )

    def relay_arrival(shift):
        here = spin_all.at[lax.rem(outer + outers - shift, outers) * PAIR + 1 - core]
        return remote(here, here, s_send.at[1, shift], s_recv.at[1, shift], {"vb": vb})

    def spin_own():
        return pltpu.make_async_copy(spin, spin_all.at[vb], own_sem.at[ratio])

    def spin_step():
        for part in range(ratio):

            @pl.when(stays(part))
            def _():
                mirror_own(part).wait()

            @pl.when(jnp.logical_not(stays(part)))
            def _():
                for half in range(halves):
                    mirror_arrival(part, half).wait_recv()

            cols = slice(part * row_len, (part + 1) * row_len)
            for i in range(halves):
                for k in range(amp_ref.shape[1]):
                    mirror = landed[part, i, k].astype(jnp.float32)
                    spin[i, k, :, cols] = (
                        2.0 * amp_ref[i, k, :, cols].astype(jnp.float32) - (mirror.T if flip else mirror)
                    ).astype(spin.dtype)
        for shift in range(1, outers):
            spin_send(shift).start()
        spin_relay(0).start()
        spin_own().start()

    spin_after = 1
    for step in range(1, lines):
        line_step(step)
        if step == spin_after:
            spin_step()
    if spin_after == 0:
        spin_step()
    for shift in range(1, outers):
        spin_arrival(shift).wait_recv()
        spin_relay(shift).start()

    for chunk in range(chunks + 1):
        if chunk < chunks:
            own_copy(chunk).wait()
            side_send(0, 0, chunk).wait_send()
            if chunk != early:
                side_arrival(0, 0, chunk).wait_recv()
        for direction in range(2):

            @pl.when(may_send(direction, 0))
            def _():
                line_send(direction, 0, chunk).wait_send()

    for step in range(1, lines):
        for chunk in range(chunks + 1):
            for direction in range(2):

                @pl.when(may_send(direction, step))
                def _():
                    line_send(direction, step, chunk).wait_send()

                if chunk < early:

                    @pl.when(has_arrival(direction, step))
                    def _():
                        side_arrival(direction, step, chunk).wait_recv()
                        side_send(direction, step, chunk).wait_send()

    each_mirror(
        lambda part: None,
        lambda part, half: mirror_straight(part, half).wait_send(),
        lambda part, half: mirror_out(part, half).wait_send(),
    )
    each_passing(lambda part, half: mirror_on(part, half).wait_send())

    spin_own().wait()
    for shift in range(outers):
        relay_arrival(shift).wait_recv()
        spin_relay(shift).wait_send()
    for shift in range(1, outers):
        spin_send(shift).wait_send()


def gather_all(amplitudes, integrals, count_va, count_vb):
    occ_a, occ_b, row_len, col_len = amplitudes.shape
    blocks, rows, cols = integrals.shape
    chunks = blocks * SPLIT
    ratio = count_va // count_vb
    lines = count_va // PAIR
    outers = count_vb // PAIR
    flip = row_len % TILE == 0
    operands = (amplitudes, integrals)
    if not flip:
        turned = amplitudes.reshape(occ_a, occ_b, row_len, ratio, row_len)
        operands = (amplitudes, jnp.transpose(turned, (3, 0, 1, 4, 2)), integrals)
    mirror_shape = (ratio, occ_a, occ_b, row_len, row_len)
    dma = pltpu.SemaphoreType.DMA
    return pl.pallas_call(
        functools.partial(gather_kernel, count_va, count_vb, flip),
        out_shape=(
            jax.ShapeDtypeStruct((blocks, count_va * rows, cols), integrals.dtype),
            jax.ShapeDtypeStruct((count_vb, occ_a, occ_b, row_len, col_len), amplitudes.dtype),
        ),
        in_specs=[pl.BlockSpec(memory_space=pltpu.VMEM)] * (len(operands) - 1)
        + [pl.BlockSpec(memory_space=pl.ANY)],
        out_specs=(pl.BlockSpec(memory_space=pl.ANY),) * 2,
        scratch_shapes=[
            pltpu.VMEM(mirror_shape, amplitudes.dtype),
            pltpu.VMEM(mirror_shape, amplitudes.dtype),
            pltpu.VMEM(amplitudes.shape, amplitudes.dtype),
            dma((2, lines, chunks + 1)),
            dma((2, lines, chunks + 1)),
            dma((2, lines, chunks)),
            dma((2, lines, chunks)),
            dma((2, ratio, occ_a)),
            dma((ratio, occ_a)),
            dma((ratio, occ_a)),
            dma((ratio, occ_a)),
            dma((2, outers)),
            dma((2, outers)),
            dma((ratio + 1 + chunks,)),
        ],
        compiler_params=pltpu.CompilerParams(has_side_effects=True),
    )(*operands)


def cycle_kernel(at, screen, lengths, occ, *refs):
    spin_refs, k_refs = refs[:GROUP], refs[GROUP : 2 * GROUP]
    rows_ref, cols_ref, out_ref = refs[2 * GROUP :]
    slot = pl.program_id(0) * GROUP
    occ_count = out_ref.shape[0]
    count = lengths[at[0]]
    row_len = out_ref.shape[2]

    @pl.when(slot == 0)
    def _():
        out_ref[...] = jnp.zeros_like(out_ref)

    @pl.when(slot < count)
    def _():
        pairs = [(m, k) for m in range(GROUP) for k in range(occ_count)]
        live = [(slot + m < count).astype(spin_refs[0].dtype) for m in range(GROUP)]
        lefts = [
            jnp.concatenate([spin_refs[m][0, i, k] * live[m] for m, k in pairs], axis=1)
            for i in range(occ_count)
        ]
        for j in range(occ_count):
            right = jnp.concatenate([k_refs[m][k * occ_count + j] for m, k in pairs], axis=0)
            for i in range(occ_count):
                out_ref[i, j] += jnp.dot(lefts[i], right, preferred_element_type=jnp.float32)

    @pl.when(pl.program_id(0) == pl.num_programs(0) - 1)
    def _():
        vir_rows = jnp.broadcast_to(rows_ref[0], (TILE, row_len)).T[:, :1]
        for i in range(occ_count):
            for j in range(occ_count):
                bottom = (occ[i] + occ[j] - vir_rows) - cols_ref[0]
                out_ref[i, j] = out_ref[i, j] / bottom


GROUPS = 2
LAG = 6
AHEAD = 2
LATE = [(2, "out", 6), (2, "in", 4), (4, "out", 7), (4, "in", 5), (6, "in", 6), (8, "in", 7)]

OUT, IN_SIDE, IN_NEAR, IN_FAR, USE, MIRROR, LIVE, LEFT, PAIRS, ROWS = 0, 1, 2, 3, 4, 6, 8, 10, 12, 16


def bit_count(value):
    value = value - ((value >> 1) & 0x5555)
    value = (value & 0x3333) + ((value >> 2) & 0x3333)
    value = (value + (value >> 4)) & 0x0F0F
    return (value + (value >> 8)) & 0x1F


def power(place):
    return jnp.left_shift(1, place)


def bit_rank(mask, place):
    return bit_count(mask & (power(place) - 1))


def set_bits(mask, count, spare):
    places = []
    for _ in range(count):
        low = mask & -mask
        places.append(jnp.where(mask == 0, spare, bit_count(low - 1)))
        mask = mask & (mask - 1)
    return places


def row_masks(screen, lengths, count_va, slots):
    def one(m, masks):
        return tuple(
            mask | jnp.where(m < lengths[row], power(jnp.maximum(screen[row, m], 0)), 0) for row, mask in enumerate(masks)
        )

    return lax.fori_loop(0, slots, one, (jnp.int32(0),) * count_va)


def level_tiles(level, per_level):
    return ((1 << per_level) - 1) << (level * per_level)


def any_of(masks):
    return functools.reduce(lambda one, two: one | two, masks)


def link_masks(masks, levels, per_level):
    wanted = [any_of(masks[level * PAIR : (level + 1) * PAIR]) for level in range(levels)]
    half = levels // 2
    end_out, mid_out, end_in = [], [], []
    for side in range(2):
        end = 0 if side == 0 else levels - 1
        mine = range(half) if side == 0 else range(half, levels)
        end_tiles = level_tiles(end, per_level)
        end_out.append(end_tiles & any_of([wanted[l] for l in range(levels) if l != end]))
        mid_out.append(
            any_of([level_tiles(l, per_level) for l in mine]) & any_of([wanted[l] for l in range(levels) if l not in mine])
        )
        end_in.append(wanted[end] & ~end_tiles)
    return end_out, mid_out, end_in


def pair_mask(low, high, level, per_level):
    every = (1 << per_level) - 1
    return ((low >> (level * per_level)) & every) | (((high >> (level * per_level)) & every) << per_level)


def listed_kernel(caps, slots, table_ref, occ_ref, amp_ref, int_ref, rows_from, cols_from, out_ref, *refs):
    first_cap, mid_cap, end_cap, pair_cap = caps
    refs = list(refs)
    count_va = lax.axis_size("va")
    levels = count_va // PAIR
    occ_count = amp_ref.shape[0]
    own_tiles = int_ref.shape[1]
    rows = own_tiles * TILE
    cols = int_ref.shape[3]
    per_level = own_tiles * PAIR
    col_parts = cols // TILE
    units = occ_count * col_parts
    pairs = slots + slots // 2
    group = pairs // GROUPS

    near = [refs.pop(0) for _ in range(units)]
    far = [refs.pop(0) for _ in range(units)]
    out_pack = [refs.pop(0) for _ in range(units)]
    in_pack = [refs.pop(0) for _ in range(units)]
    share, sib, mirror_out, mirror_in, spin_mine, spin_other = [
        [refs.pop(0) for _ in range(PAIR)] for _ in range(6)
    ]
    (
        lefts, rights, vir_rows, part_own, part_out, part_in, table, occ, rows_ref, cols_ref, load_sem, near_sem, own_sem,
        y_send, y_recv, out_send, near_recv, far_recv, in_send, a_send, a_recv, sib_send, sib_recv, m_send, m_recv,
        x_send, x_recv, c_send, c_recv, p_send, p_recv,
    ) = refs

    va = lax.axis_index("va")
    vb = lax.axis_index("vb")
    z, y = va // PAIR, va % PAIR
    x, c = vb // PAIR, vb % PAIR
    upper = z // (levels // 2)
    inner = jnp.where(upper == 0, z, levels - 1 - z)
    toward = jnp.where(upper == 0, PAIR, -PAIR)
    end_level = jnp.where(upper == 0, 0, levels - 1)
    lead = z % PAIR
    own_at = per_level + y * own_tiles

    def remote(src, dst, send, recv, target):
        return pltpu.make_async_remote_copy(
            src_ref=src, dst_ref=dst, send_sem=send, recv_sem=recv, device_id=target, device_id_type=MESH
        )

    def tile_rows(begin):
        return pl.ds(pl.multiple_of(begin * TILE, TILE), TILE)

    def unit(u):
        return u // col_parts, pl.ds(u % col_parts * TILE, TILE)

    def y_copy(u):
        j, at = unit(u)
        return remote(
            int_ref.at[(1 - y) * occ_count + j, :, :, at], near[u].at[pl.ds(own_at, own_tiles)],
            y_send.at[u], y_recv.at[u], {"va": z * PAIR + 1 - y},
        )

    def y_arrival(u):
        here = near[u].at[pl.ds(per_level + (1 - y) * own_tiles, own_tiles)]
        return remote(here, here, y_send.at[u], y_recv.at[u], {"va": va})

    flips = [(1, 0), (0, 1), (1, 1)]

    def flipped(f):
        flip_x, flip_y = flips[f]
        return x + flip_x * (1 - 2 * x), y + flip_y * (1 - 2 * y)

    def block_tiles(at_x, at_y, side):
        return pl.ds(((at_x * PAIR + at_y) * PAIR + side) * own_tiles, own_tiles)

    def half_cols(side, half):
        return pl.ds((side * PAIR + half) * TILE, TILE)

    def share_copy(half, f, side):
        to_x, to_y = flipped(f)
        return remote(
            amp_ref.at[to_x, to_y, :, :, half_cols(side, half)], share[half].at[block_tiles(x, y, side)],
            a_send.at[half, f, side], a_recv.at[half, f, side], {"va": z * PAIR + to_y, "vb": to_x * PAIR + c},
        )

    def share_arrival(half, f, side):
        here = share[half].at[block_tiles(*flipped(f), side)]
        return remote(here, here, a_send.at[half, f, side], a_recv.at[half, f, side], {"va": va})

    def each_share(act):
        for f in range(3):
            for side in range(PAIR):
                act(f, side)

    loads = [
        pltpu.make_async_copy(src, dst, load_sem.at[n])
        for n, (src, dst) in enumerate(
            [
                (table_ref, table), (occ_ref, occ),
                (rows_from.at[va], rows_ref), (cols_from.at[vb], cols_ref),
            ]
        )
    ]

    def near_own(u):
        j, at = unit(u)
        return pltpu.make_async_copy(
            int_ref.at[y * occ_count + j, :, :, at], near[u].at[pl.ds(own_at, own_tiles)], near_sem.at[u]
        )

    def share_own(half, side):
        return pltpu.make_async_copy(
            amp_ref.at[x, y, :, :, half_cols(side, half)], share[half].at[block_tiles(x, y, side)], own_sem.at[half, side]
        )

    for load in loads:
        load.start()
    for u in range(units):
        near_own(u).start()
    for half in range(PAIR):
        for side in range(PAIR):
            share_own(half, side).start()

    barrier = pltpu.get_barrier_semaphore()
    partners = [{"vb": x * PAIR + 1 - c}]
    for f in range(3):
        to_x, to_y = flipped(f)
        partners.append({"va": z * PAIR + to_y, "vb": to_x * PAIR + c})
    for step in range(1, levels):
        partners.append({"va": lax.rem(z + step, levels) * PAIR + y})
    for partner in partners:
        pl.semaphore_signal(barrier, inc=1, device_id=partner, device_id_type=MESH)
    pl.semaphore_wait(barrier, len(partners))

    y_copy(0).start()

    for load in loads:
        load.wait()
    vir_rows[...] = jnp.broadcast_to(rows_ref[...], (TILE, rows)).T

    def out_copy(u, end):
        if end:
            here, there = out_pack[u].at[pl.ds(0, first_cap)], near[u].at[pl.ds(0, first_cap)]
            return remote(here, there, out_send.at[u], near_recv.at[u], {"va": va + toward})
        here, there = out_pack[u].at[pl.ds(0, mid_cap)], far[u].at[pl.ds(0, mid_cap)]
        return remote(here, there, out_send.at[u], far_recv.at[u], {"va": va + toward})

    def near_arrival(u):
        here = near[u].at[pl.ds(0, first_cap)]
        return remote(here, here, out_send.at[u], near_recv.at[u], {"va": va})

    def far_arrival(u, end):
        here = far[u].at[pl.ds(0, end_cap if end else mid_cap)]
        return remote(here, here, out_send.at[u], far_recv.at[u], {"va": va})

    def in_copy(u):
        here, there = in_pack[u].at[pl.ds(0, end_cap)], far[u].at[pl.ds(0, end_cap)]
        return remote(here, there, in_send.at[u], far_recv.at[u], {"va": va - toward})

    def y_wait(u):
        y_arrival(u).wait_recv()

    def share_start(half):
        each_share(lambda f, side: share_copy(half, f, side).start())

    def out_step(u):
        near_own(u).wait()
        if u:
            y_wait(u)

        @pl.when(inner == 1)
        def _():
            near_arrival(u).wait_recv()

        @functools.partial(lax.fori_loop, 0, max(first_cap, mid_cap), init_val=0)
        def _(s, carry):
            out_pack[u][s] = near[u][table[OUT, s]]
            return carry

        for end in (True, False):

            @pl.when(inner == (0 if end else 1))
            def _():
                if u >= AHEAD:
                    out_copy(u - AHEAD, end).wait_send()
                out_copy(u, end).start()

    def in_step(u):
        @pl.when(inner == 1)
        def _():
            far_arrival(u, False).wait_recv()

            @functools.partial(lax.fori_loop, 0, end_cap, init_val=0)
            def _(s, carry):
                in_pack[u][s] = jnp.where(
                    table[IN_SIDE, s] == 1, near[u][table[IN_NEAR, s]], far[u][table[IN_FAR, s]]
                )
                return carry

            in_copy(u).start()

    def sib_copy(half):
        return remote(share[half], sib[half], sib_send.at[half], sib_recv.at[half], {"vb": x * PAIR + 1 - c})

    def sib_arrival(half):
        return remote(sib[half], sib[half], sib_send.at[half], sib_recv.at[half], {"vb": vb})

    def mirror_copy(half, at_x):
        level = at_x * PAIR + c
        return remote(
            mirror_out[half].at[pl.ds(at_x * pair_cap, pair_cap)],
            mirror_in[half].at[pl.ds(z * pair_cap, pair_cap)],
            m_send.at[half, at_x], m_recv.at[half, z], {"va": level * PAIR + y},
        )

    def mirror_arrival(half, level):
        here = mirror_in[half].at[pl.ds(level * pair_cap, pair_cap)]
        return remote(here, here, m_send.at[half, 0], m_recv.at[half, level], {"va": va})

    def share_step(half):
        each_share(lambda f, side: share_arrival(half, f, side).wait_recv())
        for side in range(PAIR):
            share_own(half, side).wait()
        for at_x in range(PAIR):
            level = at_x * PAIR + c

            @functools.partial(lax.fori_loop, 0, pair_cap, init_val=0)
            def _(s, carry):
                place = table[MIRROR + at_x, s]
                side, tile = place // per_level, place % per_level
                block = (at_x * PAIR + tile // own_tiles) * PAIR + side
                mirror_out[half][at_x * pair_cap + s] = share[half][block * own_tiles + tile % own_tiles]
                return carry

            @pl.when(level != z)
            def _():
                mirror_copy(half, at_x).start()

            @pl.when(level == z)
            def _():
                mirror_in[half][pl.ds(z * pair_cap, pair_cap)] = mirror_out[half][
                    pl.ds(at_x * pair_cap, pair_cap)
                ]

        @pl.when(c != lead)
        def _():
            sib_copy(half).start()

    def spin_group(ref, g):
        return ref.at[pl.ds(g * group, group)]

    def x_copy(half, g):
        return remote(
            spin_group(spin_mine[half], g), spin_group(spin_other[half], g), x_send.at[half, g], x_recv.at[half, g],
            {"vb": (1 - x) * PAIR + c},
        )

    def x_arrival(half, g):
        here = spin_group(spin_other[half], g)
        return remote(here, here, x_send.at[half, g], x_recv.at[half, g], {"vb": vb})

    def core_copy(which, half, g):
        ref = (spin_mine, spin_other)[which][half]
        return remote(
            spin_group(ref, g), spin_group(ref, g), c_send.at[which, half, g], c_recv.at[which, half, g],
            {"vb": x * PAIR + 1 - c},
        )

    def core_arrival(which, half, g):
        here = spin_group((spin_mine, spin_other)[which][half], g)
        return remote(here, here, c_send.at[which, half, g], c_recv.at[which, half, g], {"vb": vb})

    def spin_step(half):
        @pl.when(c == lead)
        def _():
            for level in range(levels):

                @pl.when(level != z)
                def _():
                    mirror_arrival(half, level).wait_recv()

            if half == 0:
                for one in range(PAIR):
                    sib_arrival(one).wait_recv()
            for g in range(GROUPS):

                @functools.partial(lax.fori_loop, g * group, (g + 1) * group, init_val=0)
                def _(q, carry):
                    side, tile, place = table[PAIRS, q], table[PAIRS + 1, q], table[PAIRS + 2, q] * pair_cap + table[PAIRS + 3, q]
                    owner, within = tile // col_parts, tile % col_parts
                    block = ((owner // PAIR) * PAIR + side) * PAIR + within // PAIR
                    at = block * own_tiles + half
                    first, second = [
                        jnp.where(owner % PAIR == lead, share[one][at], sib[one][at]) for one in range(PAIR)
                    ]
                    own = jnp.where(within % PAIR == 0, first, second)
                    mirror = mirror_in[half][place]
                    spin = 2.0 * own.astype(jnp.float32) - mirror.astype(jnp.float32).T
                    spin_mine[half][q] = spin.astype(amp_ref.dtype)
                    return carry

                x_copy(half, g).start()
                core_copy(0, half, g).start()

    def pass_step(half):
        @pl.when(c == lead)
        def _():
            for g in range(GROUPS):
                x_arrival(half, g).wait_recv()
                core_copy(1, half, g).start()

    def left_step(half):
        @pl.when(c != lead)
        def _():
            for g in range(GROUPS):
                for which in range(2):
                    core_arrival(which, half, g).wait_recv()

        @functools.partial(lax.fori_loop, 0, PAIR * slots, init_val=0)
        def _(index, carry):
            side, m = index // slots, index % slots
            live = table[LIVE + side, m] == 1
            q = table[LEFT + side, m]
            lanes = pl.ds(pl.multiple_of(m * TILE, TILE), TILE)
            for ref, place in ((spin_mine, x), (spin_other, 1 - x)):
                value = ref[half][q]
                lefts[half, side, tile_rows(place), lanes] = jnp.where(live, value, jnp.zeros_like(value))
            return carry

    def part_copy(u, half):
        return remote(
            part_out.at[u, half], part_in.at[u, half], p_send.at[u, half], p_recv.at[u, half], {"va": z * PAIR + 1 - y}
        )

    def part_arrival(u, half):
        return remote(part_in.at[u, half], part_in.at[u, half], p_send.at[u, half], p_recv.at[u, half], {"va": va})

    def end_wait(u):
        @pl.when(inner == 0)
        def _():
            far_arrival(u, True).wait_recv()

    def gather_step(u):
        @functools.partial(lax.fori_loop, 0, PAIR * slots, init_val=0)
        def _(index, carry):
            side, m = index // slots, index % slots
            place = table[USE + side, m]
            here = jnp.minimum(place, 2 * per_level - 1)
            there = jnp.maximum(place - 2 * per_level, 0)
            rights[u, side, tile_rows(m), :] = jnp.where(place < 2 * per_level, near[u][here], far[u][there])
            return carry

    def dot_step(u, half):
        total = jnp.dot(lefts[half, 1 - y], rights[u, 1 - y], preferred_element_type=jnp.float32)
        part_out[u, half] = total.astype(part_out.dtype)
        part_copy(u, half).start()
        part_own[u, half] = jnp.dot(lefts[half, y], rights[u, y], preferred_element_type=jnp.float32)

    def final_step(u, half):
        j = u // col_parts
        at = pl.ds(pl.multiple_of(u % col_parts * TILE, TILE), TILE)
        part_arrival(u, half).wait_recv()
        part_rows = tile_rows(half)
        for i in range(occ_count):
            bottom = (occ[i] + occ[j] - vir_rows[part_rows, :]) - cols_ref[:, at]
            here = pl.ds(i * TILE, TILE)
            whole = part_own[u, half, here, :] + part_in[u, half, here, :].astype(jnp.float32)
            out_ref[i, j, part_rows, at] = whole / bottom

    def y_start(u):
        if u < units:
            y_copy(u).start()

    y_wait(0)
    share_start(0)
    y_start(1)
    out_step(0)
    share_step(0)
    share_start(1)
    y_start(2)
    out_step(1)
    y_start(3)
    share_step(1)
    y_start(4)
    out_step(2)
    in_step(0)
    y_start(5)
    out_step(3)
    in_step(1)
    y_start(6)
    spin_step(0)
    y_start(7)
    out_step(4)
    in_step(2)
    pass_step(0)
    spin_step(1)
    out_step(5)
    in_step(3)
    left_step(0)

    stages = units * PAIR
    early = units // 2

    def place_of(stage):
        first = stage < early * PAIR
        u = jnp.where(first, stage % early, stage // PAIR)
        return u, jnp.where(first, stage // early, stage % PAIR)

    actions = {stage: [] for stage in range(stages)}
    for u in range(units):
        stage = u if u < early else early * PAIR + (u - early) * PAIR
        actions[stage] += [functools.partial(end_wait, u), functools.partial(gather_step, u)]
    actions[early] = [functools.partial(pass_step, 1), functools.partial(left_step, 1), *actions[early]]
    for stage, step, u in LATE:
        actions[stage] = [functools.partial({"in": in_step, "out": out_step}[step], u), *actions[stage]]

    @functools.partial(lax.fori_loop, 0, stages, init_val=0)
    def _(stage, carry):
        for at, acts in actions.items():
            if acts:

                @pl.when(stage == at)
                def _():
                    for act in acts:
                        act()

        dot_step(*place_of(stage))

        @pl.when(stage >= LAG)
        def _():
            final_step(*place_of(stage - LAG))

        return carry

    @functools.partial(lax.fori_loop, stages - LAG, stages, init_val=0)
    def _(stage, carry):
        final_step(*place_of(stage))
        return carry

    for u in range(units):
        y_copy(u).wait_send()
        for half in range(PAIR):
            part_copy(u, half).wait_send()

        @pl.when(inner == 1)
        def _():
            in_copy(u).wait_send()

        if u >= units - AHEAD:
            for end in (True, False):

                @pl.when(inner == (0 if end else 1))
                def _():
                    out_copy(u, end).wait_send()

    for half in range(PAIR):
        each_share(lambda f, side: share_copy(half, f, side).wait_send())
        for at_x in range(PAIR):

            @pl.when(at_x * PAIR + c != z)
            def _():
                mirror_copy(half, at_x).wait_send()

        @pl.when(c != lead)
        def _():
            sib_copy(half).wait_send()

        @pl.when(c == lead)
        def _():
            for g in range(GROUPS):
                x_copy(half, g).wait_send()
                for which in range(2):
                    core_copy(which, half, g).wait_send()


def listed_all(index, caps, slots, amplitudes, integrals, occ_energy, vir_energy, table):
    first_cap, mid_cap, end_cap, pair_cap = caps
    count_va = lax.axis_size("va")
    count_vb = lax.axis_size("vb")
    occ_a, occ_b, row_len, col_len = amplitudes.shape
    blocks, rows, cols = integrals.shape
    levels = count_va // PAIR
    own_tiles = rows // TILE
    per_level = own_tiles * PAIR
    units = occ_a * (cols // TILE)
    pairs = slots + slots // 2
    kind = amplitudes.dtype
    dma = pltpu.SemaphoreType.DMA
    vmem = pltpu.VMEM
    return pl.pallas_call(
        functools.partial(listed_kernel, caps, slots),
        out_shape=jax.ShapeDtypeStruct((occ_a, occ_b, row_len, cols), jnp.float32),
        in_specs=[pl.BlockSpec(memory_space=pl.ANY)] * 6,
        out_specs=pl.BlockSpec(memory_space=vmem),
        scratch_shapes=[
            *[vmem((2 * per_level, TILE, TILE), kind)] * units,
            *[vmem((max(mid_cap, end_cap), TILE, TILE), kind)] * units,
            *[vmem((max(first_cap, mid_cap), TILE, TILE), kind)] * units,
            *[vmem((end_cap, TILE, TILE), kind)] * units,
            *[vmem((PAIR * PAIR * PAIR * own_tiles, TILE, TILE), kind)] * (2 * PAIR),
            *[vmem((PAIR * pair_cap, TILE, TILE), kind)] * PAIR,
            *[vmem((levels * pair_cap, TILE, TILE), kind)] * PAIR,
            *[vmem((pairs, TILE, TILE), kind)] * (2 * PAIR),
            vmem((PAIR, PAIR, occ_a * TILE, slots * TILE), kind),
            vmem((units, PAIR, slots * TILE, TILE), kind),
            vmem((rows, TILE), jnp.float32),
            vmem((units, PAIR, occ_a * TILE, TILE), jnp.float32),
            vmem((units, PAIR, occ_a * TILE, TILE), kind),
            vmem((units, PAIR, occ_a * TILE, TILE), kind),
            pltpu.SMEM(table.shape, table.dtype),
            pltpu.SMEM(occ_energy.shape, occ_energy.dtype),
            vmem((1, row_len), jnp.float32),
            vmem((1, cols), jnp.float32),
            dma((4,)),
            dma((units,)),
            dma((PAIR, PAIR)),
            *[dma((units,))] * 6,
            *[dma((PAIR, 3, PAIR))] * 2,
            *[dma((PAIR,))] * 2,
            dma((PAIR, PAIR)), dma((PAIR, levels)),
            *[dma((PAIR, GROUPS))] * 2,
            *[dma((2, PAIR, GROUPS))] * 2,
            *[dma((units, PAIR))] * 2,
        ],
        compiler_params=pltpu.CompilerParams(collective_id=index, has_side_effects=True, vmem_limit_bytes=60 * 2**20),
    )(
        table, occ_energy, amplitudes.reshape(occ_a, occ_b, own_tiles, TILE, col_len),
        integrals.reshape(blocks, own_tiles, TILE, cols),
        vir_energy.reshape(count_va, 1, row_len), vir_energy.reshape(count_vb, 1, cols),
    )


def fits(amplitudes, integrals, screen, count_va, count_vb):
    levels = count_va // PAIR
    rows, cols = integrals.shape[1:]
    return (
        levels == PAIR * PAIR
        and count_vb == levels
        and amplitudes.shape[0] == PAIR
        and rows == PAIR * TILE
        and cols == PAIR * rows
        and count_va * rows == ROWS * TILE
        and screen.shape[1] % 4 == 0
    )


def dense(amplitudes, integrals, occ_energy, vir_energy, screen, lengths):
    count_va = lax.axis_size("va")
    count_vb = lax.axis_size("vb")
    occ_a, occ_b, row_len, col_len = amplitudes.shape
    cols = integrals.shape[2]
    whole_k, spin_all = gather_all(amplitudes, integrals, count_va, count_vb)
    slots = screen.shape[1]
    per_shard = col_len // TILE
    at = jnp.stack([lax.axis_index("va"), lax.axis_index("vb")]).astype(jnp.int32)

    def tile_of(m, at, screen, lengths):
        return jnp.maximum(screen[at[0], jnp.minimum(m, lengths[at[0]] - 1)], 0)

    def spin_at(place, m, at, screen, lengths, occ):
        tile = tile_of(m * GROUP + place, at, screen, lengths)
        return (tile // per_shard, 0, 0, 0, tile % per_shard)

    def k_at(place, m, at, screen, lengths, occ):
        return (0, tile_of(m * GROUP + place, at, screen, lengths), 0)

    return pl.pallas_call(
        cycle_kernel,
        out_shape=jax.ShapeDtypeStruct((occ_a, occ_b, row_len, cols), jnp.float32),
        grid_spec=pltpu.PrefetchScalarGridSpec(
            num_scalar_prefetch=4,
            grid=(pl.cdiv(slots, GROUP),),
            in_specs=[
                *(
                    pl.BlockSpec((1, occ_a, occ_b, row_len, TILE), functools.partial(spin_at, place))
                    for place in range(GROUP)
                ),
                *(
                    pl.BlockSpec((integrals.shape[0], TILE, cols), functools.partial(k_at, place))
                    for place in range(GROUP)
                ),
                pl.BlockSpec((1, 1, row_len), lambda m, at, screen, lengths, occ: (at[0], 0, 0)),
                pl.BlockSpec((1, 1, cols), lambda m, at, screen, lengths, occ: (at[1], 0, 0)),
            ],
            out_specs=pl.BlockSpec(
                (occ_a, occ_b, row_len, cols), lambda m, at, screen, lengths, occ: (0, 0, 0, 0)
            ),
        ),
    )(
        at, screen, lengths, occ_energy, *[spin_all] * GROUP, *[whole_k] * GROUP,
        vir_energy.reshape(count_va, 1, row_len), vir_energy.reshape(count_vb, 1, cols),
    )


CAPS = ((4, 6, 6, 4), (4, 6, 6, 5), (4, 7, 7, 4), (4, 8, 8, 5), (4, 8, 9, 6), (4, 8, 12, 8))


def plan_kernel(caps, per_level, screen_ref, lengths_ref, choice, table, screen, lengths, load_sem):
    loads = [
        pltpu.make_async_copy(src, dst, load_sem.at[n])
        for n, (src, dst) in enumerate([(screen_ref, screen), (lengths_ref, lengths)])
    ]
    for load in loads:
        load.start()
    for load in loads:
        load.wait()
    count_va, slots = screen.shape
    levels = count_va // PAIR
    tiles = levels * per_level
    pairs = slots + slots // 2
    z = lax.axis_index("va") // PAIR
    c = lax.axis_index("vb") % PAIR
    upper = z // (levels // 2)
    inner = jnp.where(upper == 0, z, levels - 1 - z)
    end_level = jnp.where(upper == 0, 0, levels - 1)

    masks = row_masks(screen, lengths, count_va, slots)
    end_out, mid_out, end_in = [
        (jnp.where(upper == 0, one[0], one[1]), jnp.where(upper == 0, one[1], one[0]))
        for one in link_masks(masks, levels, per_level)
    ]

    arrives = jnp.where(inner == 1, mid_out[1], end_in[0])

    def place_of(tile):
        level = tile // per_level
        own = level == z
        from_end = jnp.logical_and(inner == 1, level == end_level)
        rank = bit_rank(jnp.where(from_end, end_out[0], arrives), tile)
        is_near = jnp.logical_or(own, from_end)
        return is_near, jnp.where(own, per_level + tile % per_level, rank)

    spare = z * per_level
    for s, tile in enumerate(set_bits(jnp.where(inner == 1, mid_out[0], end_out[0]), per_level * PAIR, spare)):
        table[OUT, s] = place_of(tile)[1]
    for s, tile in enumerate(set_bits(end_in[0], tiles - per_level, spare)):
        is_near, place = place_of(tile)
        table[IN_SIDE, s] = is_near.astype(jnp.int32)
        table[IN_NEAR, s] = jnp.where(is_near, place, per_level)
        table[IN_FAR, s] = jnp.where(is_near, 0, place)

    def of_level(level, side):
        mask = masks[side]
        for l in range(1, levels):
            mask = jnp.where(level == l, masks[l * PAIR + side], mask)
        return mask

    for at_x in range(PAIR):
        level = at_x * PAIR + c
        mask = pair_mask(of_level(level, 0), of_level(level, 1), z, per_level)
        for s, place in enumerate(set_bits(mask, per_level * PAIR, 0)):
            table[MIRROR + at_x, s] = place

    own_masks = [of_level(z, side) for side in range(PAIR)]
    counts = [lengths[z * PAIR + side] for side in range(PAIR)]

    def own_count(side):
        return jnp.where(side == 0, counts[0], counts[1])

    @functools.partial(lax.fori_loop, 0, pairs, init_val=0)
    def _(q, carry):
        side = (q >= counts[0]).astype(jnp.int32)
        m = jnp.clip(jnp.where(side == 0, q, q - counts[0]), 0, slots - 1)
        tile = jnp.maximum(screen[z * PAIR + side, m], 0)
        level = tile // per_level
        mask = pair_mask(own_masks[0], own_masks[1], level, per_level)
        rank = bit_rank(mask, side * per_level + tile % per_level)
        table[PAIRS, q] = side
        table[PAIRS + 1, q] = tile
        table[PAIRS + 2, q] = level
        table[PAIRS + 3, q] = rank
        return carry

    @functools.partial(lax.fori_loop, 0, PAIR * slots, init_val=0)
    def _(index, carry):
        side, m = index // slots, index % slots
        tile = jnp.maximum(screen[z * PAIR + side, jnp.clip(own_count(side) - 1, 0, m)], 0)
        is_near, place = place_of(tile)
        table[USE + side, m] = jnp.where(is_near, place, 2 * per_level + place)
        table[LIVE + side, m] = (m < own_count(side)).astype(jnp.int32)
        table[LEFT + side, m] = jnp.minimum(jnp.where(side == 0, m, counts[0] + m), pairs - 1)
        return carry

    middle = jnp.maximum(*map(bit_count, mid_out))
    ends = jnp.maximum(*map(bit_count, end_in))
    most = functools.reduce(
        jnp.maximum,
        [
            bit_count(pair_mask(masks[PAIR * to], masks[PAIR * to + 1], level, per_level))
            for to in range(levels)
            for level in range(levels)
        ],
    )
    chosen = jnp.int32(len(caps) - 1)
    for index, (_, mid_cap, end_cap, pair_cap) in reversed(list(enumerate(caps[:-1]))):
        enough = jnp.logical_and(jnp.logical_and(middle <= mid_cap, ends <= end_cap), most <= pair_cap)
        chosen = jnp.where(enough, index, chosen)
    choice[0] = chosen


def plan(screen, lengths, per_level):
    return pl.pallas_call(
        functools.partial(plan_kernel, CAPS, per_level),
        out_shape=(jax.ShapeDtypeStruct((1,), jnp.int32), jax.ShapeDtypeStruct((ROWS, ROWS), jnp.int32)),
        in_specs=[pl.BlockSpec(memory_space=pl.ANY)] * 2,
        out_specs=(pl.BlockSpec(memory_space=pltpu.SMEM),) * 2,
        scratch_shapes=[
            pltpu.SMEM(screen.shape, screen.dtype),
            pltpu.SMEM(lengths.shape, lengths.dtype),
            pltpu.SemaphoreType.DMA((2,)),
        ],
        compiler_params=pltpu.CompilerParams(vmem_limit_bytes=60 * 2**20),
    )(screen, lengths)


def local(amplitudes, integrals, occ_energy, vir_energy, screen, lengths):
    operands = (amplitudes, integrals, occ_energy, vir_energy, screen, lengths)
    if not fits(amplitudes, integrals, screen, lax.axis_size("va"), lax.axis_size("vb")):
        return dense(*operands)
    choice, table = plan(screen, lengths, integrals.shape[1] // TILE * PAIR)
    branches = [functools.partial(listed_all, index, caps, screen.shape[1]) for index, caps in enumerate(CAPS)]
    return lax.switch(choice[0], branches, amplitudes, integrals, occ_energy, vir_energy, table)


def solution(mesh):
    return jax.shard_map(
        local,
        mesh=mesh,
        in_specs=(P(None, None, "va", "vb"), P(None, "va", "vb"), P(), P(), P(), P()),
        out_specs=P(None, None, "va", "vb"),
        check_vma=False,
    )
```

```python
import functools

import jax
import jax.numpy as jnp
from jax import lax
from jax.experimental import pallas as pl
from jax.experimental.pallas import tpu as pltpu
from jax.sharding import PartitionSpec as P

TILE = 128
PAIR = 2
SPLIT = 2
GROUP = 2
MESH = pl.DeviceIdType.MESH


def gather_kernel(
    count_va, count_vb, flip, amp_ref, *refs
):
    refs = list(refs)
    turned_ref = None if flip else refs.pop(0)
    (
        int_ref, whole_k, spin_all,
        landed, passing, spin, z_send, z_recv, y_send, y_recv, m_send, m_recv, x_send, x_recv, s_send, s_recv, own_sem,
    ) = refs
    va = lax.axis_index("va")
    vb = lax.axis_index("vb")
    ratio = count_va // count_vb
    lines = count_va // PAIR
    outers = count_vb // PAIR
    line, side = va // PAIR, va % PAIR
    outer, core = vb // PAIR, vb % PAIR
    blocks, rows, _ = int_ref.shape
    part_rows = rows // SPLIT
    chunks = blocks * SPLIT
    early = chunks - 1
    halves = amp_ref.shape[0]
    row_len = amp_ref.shape[2]

    def k_slot(owner, chunk):
        begin = owner * rows + chunk % SPLIT * part_rows
        return whole_k.at[chunk // SPLIT, pl.ds(pl.multiple_of(begin, part_rows), part_rows)]

    def own_slot(chunk):
        return int_ref.at[chunk // SPLIT, pl.ds(chunk % SPLIT * part_rows, part_rows)]

    def remote(src, dst, send, recv, target):
        return pltpu.make_async_remote_copy(
            src_ref=src, dst_ref=dst, send_sem=send, recv_sem=recv, device_id=target, device_id_type=MESH
        )

    next_vb = lax.rem(outer + 1, outers) * PAIR + core
    last_vb = lax.rem(outer + outers - 1, outers) * PAIR + core

    def by_relay(half):
        return outers > 1 and half % 2 == 1

    def piece(part):
        if flip:
            return amp_ref.at[:, :, :, pl.ds(part * row_len, row_len)]
        return turned_ref.at[part]

    def half_piece(part, half):
        if flip:
            return amp_ref.at[half, :, :, pl.ds(part * row_len, row_len)]
        return turned_ref.at[part, half]

    def mirror_own(part):
        return pltpu.make_async_copy(piece(part), landed.at[part], own_sem.at[part])

    def mirror_straight(part, half):
        return remote(
            half_piece(part, half), landed.at[va % ratio, half],
            m_send.at[0, part, half], m_recv.at[va % ratio, half],
            {"va": vb * ratio + part, "vb": va // ratio},
        )

    def mirror_out(part, half):
        return remote(
            half_piece(part, half), passing.at[part, half],
            x_send.at[part, half], x_recv.at[part, half], {"vb": next_vb},
        )

    def mirror_on(part, half):
        return remote(
            passing.at[part, half], landed.at[va % ratio, half],
            m_send.at[1, part, half], m_recv.at[va % ratio, half],
            {"va": last_vb * ratio + part, "vb": va // ratio},
        )

    def mirror_passing(part, half):
        here = passing.at[part, half]
        return remote(here, here, x_send.at[part, half], x_recv.at[part, half], {"vb": vb})

    def mirror_arrival(part, half):
        here = landed.at[part, half]
        return remote(here, here, m_send.at[0, part, half], m_recv.at[part, half], {"vb": vb})

    def stays(part):
        return va == vb * ratio + part

    def last_stays(part):
        return va == last_vb * ratio + part

    def each_mirror(own, straight, out):
        for part in range(ratio):

            @pl.when(stays(part))
            def _():
                own(part)

            @pl.when(jnp.logical_not(stays(part)))
            def _():
                for half in range(halves):
                    (out if by_relay(half) else straight)(part, half)

    each_mirror(
        lambda part: mirror_own(part).start(),
        lambda part, half: mirror_straight(part, half).start(),
        lambda part, half: mirror_out(part, half).start(),
    )

    def each_passing(act):
        for part in range(ratio):

            @pl.when(jnp.logical_not(last_stays(part)))
            def _():
                for half in range(halves):
                    if by_relay(half):
                        act(part, half)

    def source(direction, step):
        return line - step if direction == 0 else line + step

    def line_slot(direction, step, chunk):
        if chunk == chunks:
            return k_slot(source(direction, step) * PAIR + 1 - side, early)
        return k_slot(source(direction, step) * PAIR + side, chunk)

    def block_at(direction, step, chunk):
        if step == 0 and chunk < chunks:
            return own_slot(chunk)
        return line_slot(direction, step, chunk)

    def line_send(direction, step, chunk):
        to = line + 1 if direction == 0 else line - 1
        return remote(
            block_at(direction, step, chunk),
            line_slot(direction, step, chunk),
            z_send.at[direction, step, chunk],
            z_recv.at[direction, step, chunk],
            {"va": to * PAIR + side},
        )

    def line_arrival(direction, step, chunk):
        here = line_slot(direction, step, chunk)
        return remote(
            here, here, z_send.at[direction, step - 1, chunk], z_recv.at[direction, step - 1, chunk],
            {"va": va},
        )

    def may_send(direction, step):
        if direction == 0:
            return jnp.logical_and(line - step >= 0, line + 1 < lines)
        return jnp.logical_and(line + step < lines, line - 1 >= 0)

    def has_arrival(direction, step):
        return line - step >= 0 if direction == 0 else line + step < lines

    def side_send(direction, step, chunk):
        return remote(
            block_at(direction, step, chunk),
            line_slot(direction, step, chunk),
            y_send.at[direction, step, chunk],
            y_recv.at[direction, step, chunk],
            {"va": line * PAIR + 1 - side},
        )

    def side_arrival(direction, step, chunk):
        here = k_slot(source(direction, step) * PAIR + 1 - side, chunk)
        return remote(
            here, here, y_send.at[direction, step, chunk], y_recv.at[direction, step, chunk], {"va": va}
        )

    def own_copy(chunk):
        return pltpu.make_async_copy(own_slot(chunk), k_slot(va, chunk), own_sem.at[ratio + 1 + chunk])

    def send_own(chunk):
        for direction in range(2):

            @pl.when(may_send(direction, 0))
            def _():
                line_send(direction, 0, chunk).start()

    side_send(0, 0, early).start()
    for chunk in range(chunks):
        send_own(chunk)
        if chunk != early:
            side_send(0, 0, chunk).start()
    for chunk in range(chunks):
        own_copy(chunk).start()
    side_arrival(0, 0, early).wait_recv()
    send_own(chunks)

    def pass_mirror(part, half):
        mirror_passing(part, half).wait_recv()
        mirror_on(part, half).start()

    each_passing(pass_mirror)

    def line_step(step):
        for chunk in range(chunks + 1):
            for direction in range(2):

                @pl.when(has_arrival(direction, step))
                def _():
                    line_arrival(direction, step, chunk).wait_recv()

                    @pl.when(may_send(direction, step))
                    def _():
                        line_send(direction, step, chunk).start()

                    if chunk < early:
                        side_send(direction, step, chunk).start()

    def spin_send(shift):
        to = lax.rem(outer + shift, outers)
        return remote(
            spin, spin_all.at[vb], s_send.at[0, shift], s_recv.at[0, shift], {"vb": to * PAIR + core}
        )

    def spin_arrival(shift):
        here = spin_all.at[lax.rem(outer + outers - shift, outers) * PAIR + core]
        return remote(here, here, s_send.at[0, shift], s_recv.at[0, shift], {"vb": vb})

    def spin_relay(shift):
        held = spin_all.at[lax.rem(outer + outers - shift, outers) * PAIR + core]
        src = spin if shift == 0 else held
        return remote(
            src, held, s_send.at[1, shift], s_recv.at[1, shift], {"vb": outer * PAIR + 1 - core}
        )

    def relay_arrival(shift):
        here = spin_all.at[lax.rem(outer + outers - shift, outers) * PAIR + 1 - core]
        return remote(here, here, s_send.at[1, shift], s_recv.at[1, shift], {"vb": vb})

    def spin_own():
        return pltpu.make_async_copy(spin, spin_all.at[vb], own_sem.at[ratio])

    def spin_step():
        for part in range(ratio):

            @pl.when(stays(part))
            def _():
                mirror_own(part).wait()

            @pl.when(jnp.logical_not(stays(part)))
            def _():
                for half in range(halves):
                    mirror_arrival(part, half).wait_recv()

            cols = slice(part * row_len, (part + 1) * row_len)
            for i in range(halves):
                for k in range(amp_ref.shape[1]):
                    mirror = landed[part, i, k].astype(jnp.float32)
                    spin[i, k, :, cols] = (
                        2.0 * amp_ref[i, k, :, cols].astype(jnp.float32) - (mirror.T if flip else mirror)
                    ).astype(spin.dtype)
        for shift in range(1, outers):
            spin_send(shift).start()
        spin_relay(0).start()
        spin_own().start()

    spin_after = 1
    for step in range(1, lines):
        line_step(step)
        if step == spin_after:
            spin_step()
    if spin_after == 0:
        spin_step()
    for shift in range(1, outers):
        spin_arrival(shift).wait_recv()
        spin_relay(shift).start()

    for chunk in range(chunks + 1):
        if chunk < chunks:
            own_copy(chunk).wait()
            side_send(0, 0, chunk).wait_send()
            if chunk != early:
                side_arrival(0, 0, chunk).wait_recv()
        for direction in range(2):

            @pl.when(may_send(direction, 0))
            def _():
                line_send(direction, 0, chunk).wait_send()

    for step in range(1, lines):
        for chunk in range(chunks + 1):
            for direction in range(2):

                @pl.when(may_send(direction, step))
                def _():
                    line_send(direction, step, chunk).wait_send()

                if chunk < early:

                    @pl.when(has_arrival(direction, step))
                    def _():
                        side_arrival(direction, step, chunk).wait_recv()
                        side_send(direction, step, chunk).wait_send()

    each_mirror(
        lambda part: None,
        lambda part, half: mirror_straight(part, half).wait_send(),
        lambda part, half: mirror_out(part, half).wait_send(),
    )
    each_passing(lambda part, half: mirror_on(part, half).wait_send())

    spin_own().wait()
    for shift in range(outers):
        relay_arrival(shift).wait_recv()
        spin_relay(shift).wait_send()
    for shift in range(1, outers):
        spin_send(shift).wait_send()


def gather_all(amplitudes, integrals, count_va, count_vb):
    occ_a, occ_b, row_len, col_len = amplitudes.shape
    blocks, rows, cols = integrals.shape
    chunks = blocks * SPLIT
    ratio = count_va // count_vb
    lines = count_va // PAIR
    outers = count_vb // PAIR
    flip = row_len % TILE == 0
    operands = (amplitudes, integrals)
    if not flip:
        turned = amplitudes.reshape(occ_a, occ_b, row_len, ratio, row_len)
        operands = (amplitudes, jnp.transpose(turned, (3, 0, 1, 4, 2)), integrals)
    mirror_shape = (ratio, occ_a, occ_b, row_len, row_len)
    dma = pltpu.SemaphoreType.DMA
    return pl.pallas_call(
        functools.partial(gather_kernel, count_va, count_vb, flip),
        out_shape=(
            jax.ShapeDtypeStruct((blocks, count_va * rows, cols), integrals.dtype),
            jax.ShapeDtypeStruct((count_vb, occ_a, occ_b, row_len, col_len), amplitudes.dtype),
        ),
        in_specs=[pl.BlockSpec(memory_space=pltpu.VMEM)] * (len(operands) - 1)
        + [pl.BlockSpec(memory_space=pl.ANY)],
        out_specs=(pl.BlockSpec(memory_space=pl.ANY),) * 2,
        scratch_shapes=[
            pltpu.VMEM(mirror_shape, amplitudes.dtype),
            pltpu.VMEM(mirror_shape, amplitudes.dtype),
            pltpu.VMEM(amplitudes.shape, amplitudes.dtype),
            dma((2, lines, chunks + 1)),
            dma((2, lines, chunks + 1)),
            dma((2, lines, chunks)),
            dma((2, lines, chunks)),
            dma((2, ratio, occ_a)),
            dma((ratio, occ_a)),
            dma((ratio, occ_a)),
            dma((ratio, occ_a)),
            dma((2, outers)),
            dma((2, outers)),
            dma((ratio + 1 + chunks,)),
        ],
        compiler_params=pltpu.CompilerParams(has_side_effects=True),
    )(*operands)


def cycle_kernel(at, screen, lengths, occ, *refs):
    spin_refs, k_refs = refs[:GROUP], refs[GROUP : 2 * GROUP]
    rows_ref, cols_ref, out_ref = refs[2 * GROUP :]
    slot = pl.program_id(0) * GROUP
    occ_count = out_ref.shape[0]
    count = lengths[at[0]]
    row_len = out_ref.shape[2]

    @pl.when(slot == 0)
    def _():
        out_ref[...] = jnp.zeros_like(out_ref)

    @pl.when(slot < count)
    def _():
        pairs = [(m, k) for m in range(GROUP) for k in range(occ_count)]
        live = [(slot + m < count).astype(spin_refs[0].dtype) for m in range(GROUP)]
        lefts = [
            jnp.concatenate([spin_refs[m][0, i, k] * live[m] for m, k in pairs], axis=1)
            for i in range(occ_count)
        ]
        for j in range(occ_count):
            right = jnp.concatenate([k_refs[m][k * occ_count + j] for m, k in pairs], axis=0)
            for i in range(occ_count):
                out_ref[i, j] += jnp.dot(lefts[i], right, preferred_element_type=jnp.float32)

    @pl.when(pl.program_id(0) == pl.num_programs(0) - 1)
    def _():
        vir_rows = jnp.broadcast_to(rows_ref[0], (TILE, row_len)).T[:, :1]
        for i in range(occ_count):
            for j in range(occ_count):
                bottom = (occ[i] + occ[j] - vir_rows) - cols_ref[0]
                out_ref[i, j] = out_ref[i, j] / bottom


GROUPS = 2
LAG = 6
AHEAD = 2
LATE = [(2, "out", 6), (2, "in", 4), (4, "out", 7), (4, "in", 5), (6, "in", 6), (8, "in", 7)]

OUT, IN_SIDE, IN_NEAR, IN_FAR, USE, MIRROR, LIVE, LEFT, PAIRS, ROWS = 0, 1, 2, 3, 4, 6, 8, 10, 12, 16


def bit_count(value):
    value = value - ((value >> 1) & 0x5555)
    value = (value & 0x3333) + ((value >> 2) & 0x3333)
    value = (value + (value >> 4)) & 0x0F0F
    return (value + (value >> 8)) & 0x1F


def power(place):
    return jnp.left_shift(1, place)


def bit_rank(mask, place):
    return bit_count(mask & (power(place) - 1))


def set_bits(mask, count, spare):
    places = []
    for _ in range(count):
        low = mask & -mask
        places.append(jnp.where(mask == 0, spare, bit_count(low - 1)))
        mask = mask & (mask - 1)
    return places


def row_masks(screen, lengths, count_va, slots):
    def one(m, masks):
        return tuple(
            mask | jnp.where(m < lengths[row], power(jnp.maximum(screen[row, m], 0)), 0) for row, mask in enumerate(masks)
        )

    return lax.fori_loop(0, slots, one, (jnp.int32(0),) * count_va)


def level_tiles(level, per_level):
    return ((1 << per_level) - 1) << (level * per_level)


def any_of(masks):
    return functools.reduce(lambda one, two: one | two, masks)


def link_masks(masks, levels, per_level):
    wanted = [any_of(masks[level * PAIR : (level + 1) * PAIR]) for level in range(levels)]
    half = levels // 2
    end_out, mid_out, end_in = [], [], []
    for side in range(2):
        end = 0 if side == 0 else levels - 1
        mine = range(half) if side == 0 else range(half, levels)
        end_tiles = level_tiles(end, per_level)
        end_out.append(end_tiles & any_of([wanted[l] for l in range(levels) if l != end]))
        mid_out.append(
            any_of([level_tiles(l, per_level) for l in mine]) & any_of([wanted[l] for l in range(levels) if l not in mine])
        )
        end_in.append(wanted[end] & ~end_tiles)
    return end_out, mid_out, end_in


def pair_mask(low, high, level, per_level):
    every = (1 << per_level) - 1
    return ((low >> (level * per_level)) & every) | (((high >> (level * per_level)) & every) << per_level)


def listed_kernel(caps, slots, table_ref, occ_ref, amp_ref, int_ref, rows_from, cols_from, out_ref, *refs):
    first_cap, mid_cap, end_cap, pair_cap = caps
    refs = list(refs)
    count_va = lax.axis_size("va")
    levels = count_va // PAIR
    occ_count = amp_ref.shape[0]
    own_tiles = int_ref.shape[1]
    rows = own_tiles * TILE
    cols = int_ref.shape[3]
    per_level = own_tiles * PAIR
    col_parts = cols // TILE
    units = occ_count * col_parts
    pairs = slots + slots // 2
    group = pairs // GROUPS

    near = [refs.pop(0) for _ in range(units)]
    far = [refs.pop(0) for _ in range(units)]
    out_pack = [refs.pop(0) for _ in range(units)]
    in_pack = [refs.pop(0) for _ in range(units)]
    share, sib, mirror_out, mirror_in, spin_mine, spin_other = [
        [refs.pop(0) for _ in range(PAIR)] for _ in range(6)
    ]
    (
        lefts, rights, vir_rows, part_own, part_out, part_in, table, occ, rows_ref, cols_ref, load_sem, near_sem, own_sem,
        y_send, y_recv, out_send, near_recv, far_recv, in_send, a_send, a_recv, sib_send, sib_recv, m_send, m_recv,
        x_send, x_recv, c_send, c_recv, p_send, p_recv,
    ) = refs

    va = lax.axis_index("va")
    vb = lax.axis_index("vb")
    z, y = va // PAIR, va % PAIR
    x, c = vb // PAIR, vb % PAIR
    upper = z // (levels // 2)
    inner = jnp.where(upper == 0, z, levels - 1 - z)
    toward = jnp.where(upper == 0, PAIR, -PAIR)
    end_level = jnp.where(upper == 0, 0, levels - 1)
    lead = z % PAIR
    own_at = per_level + y * own_tiles

    def remote(src, dst, send, recv, target):
        return pltpu.make_async_remote_copy(
            src_ref=src, dst_ref=dst, send_sem=send, recv_sem=recv, device_id=target, device_id_type=MESH
        )

    def tile_rows(begin):
        return pl.ds(pl.multiple_of(begin * TILE, TILE), TILE)

    def unit(u):
        return u // col_parts, pl.ds(u % col_parts * TILE, TILE)

    def y_copy(u):
        j, at = unit(u)
        return remote(
            int_ref.at[(1 - y) * occ_count + j, :, :, at], near[u].at[pl.ds(own_at, own_tiles)],
            y_send.at[u], y_recv.at[u], {"va": z * PAIR + 1 - y},
        )

    def y_arrival(u):
        here = near[u].at[pl.ds(per_level + (1 - y) * own_tiles, own_tiles)]
        return remote(here, here, y_send.at[u], y_recv.at[u], {"va": va})

    flips = [(1, 0), (0, 1), (1, 1)]

    def flipped(f):
        flip_x, flip_y = flips[f]
        return x + flip_x * (1 - 2 * x), y + flip_y * (1 - 2 * y)

    def block_tiles(at_x, at_y, side):
        return pl.ds(((at_x * PAIR + at_y) * PAIR + side) * own_tiles, own_tiles)

    def half_cols(side, half):
        return pl.ds((side * PAIR + half) * TILE, TILE)

    def share_copy(half, f, side):
        to_x, to_y = flipped(f)
        return remote(
            amp_ref.at[to_x, to_y, :, :, half_cols(side, half)], share[half].at[block_tiles(x, y, side)],
            a_send.at[half, f, side], a_recv.at[half, f, side], {"va": z * PAIR + to_y, "vb": to_x * PAIR + c},
        )

    def share_arrival(half, f, side):
        here = share[half].at[block_tiles(*flipped(f), side)]
        return remote(here, here, a_send.at[half, f, side], a_recv.at[half, f, side], {"va": va})

    def each_share(act):
        for f in range(3):
            for side in range(PAIR):
                act(f, side)

    loads = [
        pltpu.make_async_copy(src, dst, load_sem.at[n])
        for n, (src, dst) in enumerate(
            [
                (table_ref, table), (occ_ref, occ),
                (rows_from.at[va], rows_ref), (cols_from.at[vb], cols_ref),
            ]
        )
    ]

    def near_own(u):
        j, at = unit(u)
        return pltpu.make_async_copy(
            int_ref.at[y * occ_count + j, :, :, at], near[u].at[pl.ds(own_at, own_tiles)], near_sem.at[u]
        )

    def share_own(half, side):
        return pltpu.make_async_copy(
            amp_ref.at[x, y, :, :, half_cols(side, half)], share[half].at[block_tiles(x, y, side)], own_sem.at[half, side]
        )

    for load in loads:
        load.start()
    for u in range(units):
        near_own(u).start()
    for half in range(PAIR):
        for side in range(PAIR):
            share_own(half, side).start()

    barrier = pltpu.get_barrier_semaphore()
    partners = [{"vb": x * PAIR + 1 - c}]
    for f in range(3):
        to_x, to_y = flipped(f)
        partners.append({"va": z * PAIR + to_y, "vb": to_x * PAIR + c})
    for step in range(1, levels):
        partners.append({"va": lax.rem(z + step, levels) * PAIR + y})
    for partner in partners:
        pl.semaphore_signal(barrier, inc=1, device_id=partner, device_id_type=MESH)
    pl.semaphore_wait(barrier, len(partners))

    y_copy(0).start()

    for load in loads:
        load.wait()
    vir_rows[...] = jnp.broadcast_to(rows_ref[...], (TILE, rows)).T

    def out_copy(u, end):
        if end:
            here, there = out_pack[u].at[pl.ds(0, first_cap)], near[u].at[pl.ds(0, first_cap)]
            return remote(here, there, out_send.at[u], near_recv.at[u], {"va": va + toward})
        here, there = out_pack[u].at[pl.ds(0, mid_cap)], far[u].at[pl.ds(0, mid_cap)]
        return remote(here, there, out_send.at[u], far_recv.at[u], {"va": va + toward})

    def near_arrival(u):
        here = near[u].at[pl.ds(0, first_cap)]
        return remote(here, here, out_send.at[u], near_recv.at[u], {"va": va})

    def far_arrival(u, end):
        here = far[u].at[pl.ds(0, end_cap if end else mid_cap)]
        return remote(here, here, out_send.at[u], far_recv.at[u], {"va": va})

    def in_copy(u):
        here, there = in_pack[u].at[pl.ds(0, end_cap)], far[u].at[pl.ds(0, end_cap)]
        return remote(here, there, in_send.at[u], far_recv.at[u], {"va": va - toward})

    def y_wait(u):
        y_arrival(u).wait_recv()

    def share_start(half):
        each_share(lambda f, side: share_copy(half, f, side).start())

    def out_step(u):
        near_own(u).wait()
        if u:
            y_wait(u)

        @pl.when(inner == 1)
        def _():
            near_arrival(u).wait_recv()

        @functools.partial(lax.fori_loop, 0, max(first_cap, mid_cap), init_val=0)
        def _(s, carry):
            out_pack[u][s] = near[u][table[OUT, s]]
            return carry

        for end in (True, False):

            @pl.when(inner == (0 if end else 1))
            def _():
                if u >= AHEAD:
                    out_copy(u - AHEAD, end).wait_send()
                out_copy(u, end).start()

    def in_step(u):
        @pl.when(inner == 1)
        def _():
            far_arrival(u, False).wait_recv()

            @functools.partial(lax.fori_loop, 0, end_cap, init_val=0)
            def _(s, carry):
                in_pack[u][s] = jnp.where(
                    table[IN_SIDE, s] == 1, near[u][table[IN_NEAR, s]], far[u][table[IN_FAR, s]]
                )
                return carry

            in_copy(u).start()

    def sib_copy(half):
        return remote(share[half], sib[half], sib_send.at[half], sib_recv.at[half], {"vb": x * PAIR + 1 - c})

    def sib_arrival(half):
        return remote(sib[half], sib[half], sib_send.at[half], sib_recv.at[half], {"vb": vb})

    def mirror_copy(half, at_x):
        level = at_x * PAIR + c
        return remote(
            mirror_out[half].at[pl.ds(at_x * pair_cap, pair_cap)],
            mirror_in[half].at[pl.ds(z * pair_cap, pair_cap)],
            m_send.at[half, at_x], m_recv.at[half, z], {"va": level * PAIR + y},
        )

    def mirror_arrival(half, level):
        here = mirror_in[half].at[pl.ds(level * pair_cap, pair_cap)]
        return remote(here, here, m_send.at[half, 0], m_recv.at[half, level], {"va": va})

    def share_step(half):
        each_share(lambda f, side: share_arrival(half, f, side).wait_recv())
        for side in range(PAIR):
            share_own(half, side).wait()
        for at_x in range(PAIR):
            level = at_x * PAIR + c

            @functools.partial(lax.fori_loop, 0, pair_cap, init_val=0)
            def _(s, carry):
                place = table[MIRROR + at_x, s]
                side, tile = place // per_level, place % per_level
                block = (at_x * PAIR + tile // own_tiles) * PAIR + side
                mirror_out[half][at_x * pair_cap + s] = share[half][block * own_tiles + tile % own_tiles]
                return carry

            @pl.when(level != z)
            def _():
                mirror_copy(half, at_x).start()

            @pl.when(level == z)
            def _():
                mirror_in[half][pl.ds(z * pair_cap, pair_cap)] = mirror_out[half][
                    pl.ds(at_x * pair_cap, pair_cap)
                ]

        @pl.when(c != lead)
        def _():
            sib_copy(half).start()

    def spin_group(ref, g):
        return ref.at[pl.ds(g * group, group)]

    def x_copy(half, g):
        return remote(
            spin_group(spin_mine[half], g), spin_group(spin_other[half], g), x_send.at[half, g], x_recv.at[half, g],
            {"vb": (1 - x) * PAIR + c},
        )

    def x_arrival(half, g):
        here = spin_group(spin_other[half], g)
        return remote(here, here, x_send.at[half, g], x_recv.at[half, g], {"vb": vb})

    def core_copy(which, half, g):
        ref = (spin_mine, spin_other)[which][half]
        return remote(
            spin_group(ref, g), spin_group(ref, g), c_send.at[which, half, g], c_recv.at[which, half, g],
            {"vb": x * PAIR + 1 - c},
        )

    def core_arrival(which, half, g):
        here = spin_group((spin_mine, spin_other)[which][half], g)
        return remote(here, here, c_send.at[which, half, g], c_recv.at[which, half, g], {"vb": vb})

    def spin_step(half):
        @pl.when(c == lead)
        def _():
            for level in range(levels):

                @pl.when(level != z)
                def _():
                    mirror_arrival(half, level).wait_recv()

            if half == 0:
                for one in range(PAIR):
                    sib_arrival(one).wait_recv()
            for g in range(GROUPS):

                @functools.partial(lax.fori_loop, g * group, (g + 1) * group, init_val=0)
                def _(q, carry):
                    side, tile, place = table[PAIRS, q], table[PAIRS + 1, q], table[PAIRS + 2, q] * pair_cap + table[PAIRS + 3, q]
                    owner, within = tile // col_parts, tile % col_parts
                    block = ((owner // PAIR) * PAIR + side) * PAIR + within // PAIR
                    at = block * own_tiles + half
                    first, second = [
                        jnp.where(owner % PAIR == lead, share[one][at], sib[one][at]) for one in range(PAIR)
                    ]
                    own = jnp.where(within % PAIR == 0, first, second)
                    mirror = mirror_in[half][place]
                    spin = 2.0 * own.astype(jnp.float32) - mirror.astype(jnp.float32).T
                    spin_mine[half][q] = spin.astype(amp_ref.dtype)
                    return carry

                x_copy(half, g).start()
                core_copy(0, half, g).start()

    def pass_step(half):
        @pl.when(c == lead)
        def _():
            for g in range(GROUPS):
                x_arrival(half, g).wait_recv()
                core_copy(1, half, g).start()

    def left_step(half):
        @pl.when(c != lead)
        def _():
            for g in range(GROUPS):
                for which in range(2):
                    core_arrival(which, half, g).wait_recv()

        @functools.partial(lax.fori_loop, 0, PAIR * slots, init_val=0)
        def _(index, carry):
            side, m = index // slots, index % slots
            live = table[LIVE + side, m] == 1
            q = table[LEFT + side, m]
            lanes = pl.ds(pl.multiple_of(m * TILE, TILE), TILE)
            for ref, place in ((spin_mine, x), (spin_other, 1 - x)):
                value = ref[half][q]
                lefts[half, side, tile_rows(place), lanes] = jnp.where(live, value, jnp.zeros_like(value))
            return carry

    def part_copy(u, half):
        return remote(
            part_out.at[u, half], part_in.at[u, half], p_send.at[u, half], p_recv.at[u, half], {"va": z * PAIR + 1 - y}
        )

    def part_arrival(u, half):
        return remote(part_in.at[u, half], part_in.at[u, half], p_send.at[u, half], p_recv.at[u, half], {"va": va})

    def end_wait(u):
        @pl.when(inner == 0)
        def _():
            far_arrival(u, True).wait_recv()

    def gather_step(u):
        @functools.partial(lax.fori_loop, 0, PAIR * slots, init_val=0)
        def _(index, carry):
            side, m = index // slots, index % slots
            place = table[USE + side, m]
            here = jnp.minimum(place, 2 * per_level - 1)
            there = jnp.maximum(place - 2 * per_level, 0)
            rights[u, side, tile_rows(m), :] = jnp.where(place < 2 * per_level, near[u][here], far[u][there])
            return carry

    def dot_step(u, half):
        total = jnp.dot(lefts[half, 1 - y], rights[u, 1 - y], preferred_element_type=jnp.float32)
        part_out[u, half] = total.astype(part_out.dtype)
        part_copy(u, half).start()
        part_own[u, half] = jnp.dot(lefts[half, y], rights[u, y], preferred_element_type=jnp.float32)

    def final_step(u, half):
        j = u // col_parts
        at = pl.ds(pl.multiple_of(u % col_parts * TILE, TILE), TILE)
        part_arrival(u, half).wait_recv()
        part_rows = tile_rows(half)
        for i in range(occ_count):
            bottom = (occ[i] + occ[j] - vir_rows[part_rows, :]) - cols_ref[:, at]
            here = pl.ds(i * TILE, TILE)
            whole = part_own[u, half, here, :] + part_in[u, half, here, :].astype(jnp.float32)
            out_ref[i, j, part_rows, at] = whole / bottom

    def y_start(u):
        if u < units:
            y_copy(u).start()

    y_wait(0)
    share_start(0)
    y_start(1)
    out_step(0)
    share_step(0)
    share_start(1)
    y_start(2)
    out_step(1)
    y_start(3)
    share_step(1)
    y_start(4)
    out_step(2)
    in_step(0)
    y_start(5)
    out_step(3)
    in_step(1)
    y_start(6)
    spin_step(0)
    y_start(7)
    out_step(4)
    in_step(2)
    pass_step(0)
    spin_step(1)
    out_step(5)
    in_step(3)
    left_step(0)

    stages = units * PAIR
    early = units // 2

    def place_of(stage):
        first = stage < early * PAIR
        u = jnp.where(first, stage % early, stage // PAIR)
        return u, jnp.where(first, stage // early, stage % PAIR)

    actions = {stage: [] for stage in range(stages)}
    for u in range(units):
        stage = u if u < early else early * PAIR + (u - early) * PAIR
        actions[stage] += [functools.partial(end_wait, u), functools.partial(gather_step, u)]
    actions[early] = [functools.partial(pass_step, 1), functools.partial(left_step, 1), *actions[early]]
    for stage, step, u in LATE:
        actions[stage] = [functools.partial({"in": in_step, "out": out_step}[step], u), *actions[stage]]

    @functools.partial(lax.fori_loop, 0, stages, init_val=0)
    def _(stage, carry):
        for at, acts in actions.items():
            if acts:

                @pl.when(stage == at)
                def _():
                    for act in acts:
                        act()

        dot_step(*place_of(stage))

        @pl.when(stage >= LAG)
        def _():
            final_step(*place_of(stage - LAG))

        return carry

    @functools.partial(lax.fori_loop, stages - LAG, stages, init_val=0)
    def _(stage, carry):
        final_step(*place_of(stage))
        return carry

    for u in range(units):
        y_copy(u).wait_send()
        for half in range(PAIR):
            part_copy(u, half).wait_send()

        @pl.when(inner == 1)
        def _():
            in_copy(u).wait_send()

        if u >= units - AHEAD:
            for end in (True, False):

                @pl.when(inner == (0 if end else 1))
                def _():
                    out_copy(u, end).wait_send()

    for half in range(PAIR):
        each_share(lambda f, side: share_copy(half, f, side).wait_send())
        for at_x in range(PAIR):

            @pl.when(at_x * PAIR + c != z)
            def _():
                mirror_copy(half, at_x).wait_send()

        @pl.when(c != lead)
        def _():
            sib_copy(half).wait_send()

        @pl.when(c == lead)
        def _():
            for g in range(GROUPS):
                x_copy(half, g).wait_send()
                for which in range(2):
                    core_copy(which, half, g).wait_send()


def listed_all(index, caps, slots, amplitudes, integrals, occ_energy, vir_energy, table):
    first_cap, mid_cap, end_cap, pair_cap = caps
    count_va = lax.axis_size("va")
    count_vb = lax.axis_size("vb")
    occ_a, occ_b, row_len, col_len = amplitudes.shape
    blocks, rows, cols = integrals.shape
    levels = count_va // PAIR
    own_tiles = rows // TILE
    per_level = own_tiles * PAIR
    units = occ_a * (cols // TILE)
    pairs = slots + slots // 2
    kind = amplitudes.dtype
    dma = pltpu.SemaphoreType.DMA
    vmem = pltpu.VMEM
    return pl.pallas_call(
        functools.partial(listed_kernel, caps, slots),
        out_shape=jax.ShapeDtypeStruct((occ_a, occ_b, row_len, cols), jnp.float32),
        in_specs=[pl.BlockSpec(memory_space=pl.ANY)] * 6,
        out_specs=pl.BlockSpec(memory_space=vmem),
        scratch_shapes=[
            *[vmem((2 * per_level, TILE, TILE), kind)] * units,
            *[vmem((max(mid_cap, end_cap), TILE, TILE), kind)] * units,
            *[vmem((max(first_cap, mid_cap), TILE, TILE), kind)] * units,
            *[vmem((end_cap, TILE, TILE), kind)] * units,
            *[vmem((PAIR * PAIR * PAIR * own_tiles, TILE, TILE), kind)] * (2 * PAIR),
            *[vmem((PAIR * pair_cap, TILE, TILE), kind)] * PAIR,
            *[vmem((levels * pair_cap, TILE, TILE), kind)] * PAIR,
            *[vmem((pairs, TILE, TILE), kind)] * (2 * PAIR),
            vmem((PAIR, PAIR, occ_a * TILE, slots * TILE), kind),
            vmem((units, PAIR, slots * TILE, TILE), kind),
            vmem((rows, TILE), jnp.float32),
            vmem((units, PAIR, occ_a * TILE, TILE), jnp.float32),
            vmem((units, PAIR, occ_a * TILE, TILE), kind),
            vmem((units, PAIR, occ_a * TILE, TILE), kind),
            pltpu.SMEM(table.shape, table.dtype),
            pltpu.SMEM(occ_energy.shape, occ_energy.dtype),
            vmem((1, row_len), jnp.float32),
            vmem((1, cols), jnp.float32),
            dma((4,)),
            dma((units,)),
            dma((PAIR, PAIR)),
            *[dma((units,))] * 6,
            *[dma((PAIR, 3, PAIR))] * 2,
            *[dma((PAIR,))] * 2,
            dma((PAIR, PAIR)), dma((PAIR, levels)),
            *[dma((PAIR, GROUPS))] * 2,
            *[dma((2, PAIR, GROUPS))] * 2,
            *[dma((units, PAIR))] * 2,
        ],
        compiler_params=pltpu.CompilerParams(collective_id=index, has_side_effects=True, vmem_limit_bytes=60 * 2**20),
    )(
        table, occ_energy, amplitudes.reshape(occ_a, occ_b, own_tiles, TILE, col_len),
        integrals.reshape(blocks, own_tiles, TILE, cols),
        vir_energy.reshape(count_va, 1, row_len), vir_energy.reshape(count_vb, 1, cols),
    )


def fits(amplitudes, integrals, screen, count_va, count_vb):
    levels = count_va // PAIR
    rows, cols = integrals.shape[1:]
    return (
        levels == PAIR * PAIR
        and count_vb == levels
        and amplitudes.shape[0] == PAIR
        and rows == PAIR * TILE
        and cols == PAIR * rows
        and count_va * rows == ROWS * TILE
        and screen.shape[1] % 4 == 0
    )


def dense(amplitudes, integrals, occ_energy, vir_energy, screen, lengths):
    count_va = lax.axis_size("va")
    count_vb = lax.axis_size("vb")
    occ_a, occ_b, row_len, col_len = amplitudes.shape
    cols = integrals.shape[2]
    whole_k, spin_all = gather_all(amplitudes, integrals, count_va, count_vb)
    slots = screen.shape[1]
    per_shard = col_len // TILE
    at = jnp.stack([lax.axis_index("va"), lax.axis_index("vb")]).astype(jnp.int32)

    def tile_of(m, at, screen, lengths):
        return jnp.maximum(screen[at[0], jnp.minimum(m, lengths[at[0]] - 1)], 0)

    def spin_at(place, m, at, screen, lengths, occ):
        tile = tile_of(m * GROUP + place, at, screen, lengths)
        return (tile // per_shard, 0, 0, 0, tile % per_shard)

    def k_at(place, m, at, screen, lengths, occ):
        return (0, tile_of(m * GROUP + place, at, screen, lengths), 0)

    return pl.pallas_call(
        cycle_kernel,
        out_shape=jax.ShapeDtypeStruct((occ_a, occ_b, row_len, cols), jnp.float32),
        grid_spec=pltpu.PrefetchScalarGridSpec(
            num_scalar_prefetch=4,
            grid=(pl.cdiv(slots, GROUP),),
            in_specs=[
                *(
                    pl.BlockSpec((1, occ_a, occ_b, row_len, TILE), functools.partial(spin_at, place))
                    for place in range(GROUP)
                ),
                *(
                    pl.BlockSpec((integrals.shape[0], TILE, cols), functools.partial(k_at, place))
                    for place in range(GROUP)
                ),
                pl.BlockSpec((1, 1, row_len), lambda m, at, screen, lengths, occ: (at[0], 0, 0)),
                pl.BlockSpec((1, 1, cols), lambda m, at, screen, lengths, occ: (at[1], 0, 0)),
            ],
            out_specs=pl.BlockSpec(
                (occ_a, occ_b, row_len, cols), lambda m, at, screen, lengths, occ: (0, 0, 0, 0)
            ),
        ),
    )(
        at, screen, lengths, occ_energy, *[spin_all] * GROUP, *[whole_k] * GROUP,
        vir_energy.reshape(count_va, 1, row_len), vir_energy.reshape(count_vb, 1, cols),
    )


CAPS = ((4, 6, 6, 4), (4, 6, 6, 5), (4, 7, 7, 4), (4, 7, 7, 5), (4, 8, 8, 5), (4, 8, 9, 6), (4, 8, 12, 8))


def plan_kernel(caps, per_level, screen_ref, lengths_ref, choice, table, screen, lengths, load_sem):
    loads = [
        pltpu.make_async_copy(src, dst, load_sem.at[n])
        for n, (src, dst) in enumerate([(screen_ref, screen), (lengths_ref, lengths)])
    ]
    for load in loads:
        load.start()
    for load in loads:
        load.wait()
    count_va, slots = screen.shape
    levels = count_va // PAIR
    tiles = levels * per_level
    pairs = slots + slots // 2
    z = lax.axis_index("va") // PAIR
    c = lax.axis_index("vb") % PAIR
    upper = z // (levels // 2)
    inner = jnp.where(upper == 0, z, levels - 1 - z)
    end_level = jnp.where(upper == 0, 0, levels - 1)

    masks = row_masks(screen, lengths, count_va, slots)
    end_out, mid_out, end_in = [
        (jnp.where(upper == 0, one[0], one[1]), jnp.where(upper == 0, one[1], one[0]))
        for one in link_masks(masks, levels, per_level)
    ]

    arrives = jnp.where(inner == 1, mid_out[1], end_in[0])

    def place_of(tile):
        level = tile // per_level
        own = level == z
        from_end = jnp.logical_and(inner == 1, level == end_level)
        rank = bit_rank(jnp.where(from_end, end_out[0], arrives), tile)
        is_near = jnp.logical_or(own, from_end)
        return is_near, jnp.where(own, per_level + tile % per_level, rank)

    spare = z * per_level
    for s, tile in enumerate(set_bits(jnp.where(inner == 1, mid_out[0], end_out[0]), per_level * PAIR, spare)):
        table[OUT, s] = place_of(tile)[1]
    for s, tile in enumerate(set_bits(end_in[0], tiles - per_level, spare)):
        is_near, place = place_of(tile)
        table[IN_SIDE, s] = is_near.astype(jnp.int32)
        table[IN_NEAR, s] = jnp.where(is_near, place, per_level)
        table[IN_FAR, s] = jnp.where(is_near, 0, place)

    def of_level(level, side):
        mask = masks[side]
        for l in range(1, levels):
            mask = jnp.where(level == l, masks[l * PAIR + side], mask)
        return mask

    for at_x in range(PAIR):
        level = at_x * PAIR + c
        mask = pair_mask(of_level(level, 0), of_level(level, 1), z, per_level)
        for s, place in enumerate(set_bits(mask, per_level * PAIR, 0)):
            table[MIRROR + at_x, s] = place

    own_masks = [of_level(z, side) for side in range(PAIR)]
    counts = [lengths[z * PAIR + side] for side in range(PAIR)]

    def own_count(side):
        return jnp.where(side == 0, counts[0], counts[1])

    @functools.partial(lax.fori_loop, 0, pairs, init_val=0)
    def _(q, carry):
        side = (q >= counts[0]).astype(jnp.int32)
        m = jnp.clip(jnp.where(side == 0, q, q - counts[0]), 0, slots - 1)
        tile = jnp.maximum(screen[z * PAIR + side, m], 0)
        level = tile // per_level
        mask = pair_mask(own_masks[0], own_masks[1], level, per_level)
        rank = bit_rank(mask, side * per_level + tile % per_level)
        table[PAIRS, q] = side
        table[PAIRS + 1, q] = tile
        table[PAIRS + 2, q] = level
        table[PAIRS + 3, q] = rank
        return carry

    @functools.partial(lax.fori_loop, 0, PAIR * slots, init_val=0)
    def _(index, carry):
        side, m = index // slots, index % slots
        tile = jnp.maximum(screen[z * PAIR + side, jnp.clip(own_count(side) - 1, 0, m)], 0)
        is_near, place = place_of(tile)
        table[USE + side, m] = jnp.where(is_near, place, 2 * per_level + place)
        table[LIVE + side, m] = (m < own_count(side)).astype(jnp.int32)
        table[LEFT + side, m] = jnp.minimum(jnp.where(side == 0, m, counts[0] + m), pairs - 1)
        return carry

    middle = jnp.maximum(*map(bit_count, mid_out))
    ends = jnp.maximum(*map(bit_count, end_in))
    most = functools.reduce(
        jnp.maximum,
        [
            bit_count(pair_mask(masks[PAIR * to], masks[PAIR * to + 1], level, per_level))
            for to in range(levels)
            for level in range(levels)
        ],
    )
    chosen = jnp.int32(len(caps) - 1)
    for index, (_, mid_cap, end_cap, pair_cap) in reversed(list(enumerate(caps[:-1]))):
        enough = jnp.logical_and(jnp.logical_and(middle <= mid_cap, ends <= end_cap), most <= pair_cap)
        chosen = jnp.where(enough, index, chosen)
    choice[0] = chosen


def plan(screen, lengths, per_level):
    return pl.pallas_call(
        functools.partial(plan_kernel, CAPS, per_level),
        out_shape=(jax.ShapeDtypeStruct((1,), jnp.int32), jax.ShapeDtypeStruct((ROWS, ROWS), jnp.int32)),
        in_specs=[pl.BlockSpec(memory_space=pl.ANY)] * 2,
        out_specs=(pl.BlockSpec(memory_space=pltpu.SMEM),) * 2,
        scratch_shapes=[
            pltpu.SMEM(screen.shape, screen.dtype),
            pltpu.SMEM(lengths.shape, lengths.dtype),
            pltpu.SemaphoreType.DMA((2,)),
        ],
        compiler_params=pltpu.CompilerParams(vmem_limit_bytes=60 * 2**20),
    )(screen, lengths)


def local(amplitudes, integrals, occ_energy, vir_energy, screen, lengths):
    operands = (amplitudes, integrals, occ_energy, vir_energy, screen, lengths)
    if not fits(amplitudes, integrals, screen, lax.axis_size("va"), lax.axis_size("vb")):
        return dense(*operands)
    choice, table = plan(screen, lengths, integrals.shape[1] // TILE * PAIR)
    branches = [functools.partial(listed_all, index, caps, screen.shape[1]) for index, caps in enumerate(CAPS)]
    return lax.switch(choice[0], branches, amplitudes, integrals, occ_energy, vir_energy, table)


def solution(mesh):
    return jax.shard_map(
        local,
        mesh=mesh,
        in_specs=(P(None, None, "va", "vb"), P(None, "va", "vb"), P(), P(), P(), P()),
        out_specs=P(None, None, "va", "vb"),
        check_vma=False,
    )
```
